32 devices in a mesh: tm: 8 (over y, x, core), seq: 4 (over z).
Axes of the slice: x: 2, y: 2, z: 4, core: 2. Of those that a mesh axis runs over, the one named last changes fastest.
Arguments:
- latents: bfloat16 [32, 16, 2048], P('tm', None, 'seq'), may hold values from -6 to 6
- hidden: bfloat16 [16384, 3072], P(('tm', 'seq')), may hold values from -6 to 6
- grad_out: bfloat16 [32, 512, 2048], P('tm', None, 'seq'), may hold values from -6 to 6
- conv_in_w: bfloat16 [3, 512, 16], replicated, may hold values from -0.875 to 0.875
- conv_in_b: float32 [512], replicated, may hold values from -4 to 4
- conv_w: bfloat16 [3, 512, 512], replicated, may hold values from -0.15625 to 0.15625
- final_w: bfloat16 [3072, 64], replicated, may hold values from -0.109375 to 0.109375
- modulation: float32 [2, 3072], replicated, may hold values from -3 to 3
- clip_start: int32 [32], replicated, may hold values from 0 to 31, as said below
Outputs:
- hidden_input_gradient: bfloat16 [16384, 3072], P(('tm', 'seq'))
- convolution_weight_gradient: float32 [512, 3, 512], P(('tm', 'seq'))
- input_convolution_gradient: float32 [3, 512, 16], replicated
- input_bias_gradient: float32 [512], replicated
- final_grad: float32 [3072, 64], replicated
- modulation_grad: float32 [2, 3072], replicated
The draws below stay inside these ranges and needn't reach their ends.
Inputs may be any that keep to these rules, and one draw needn't show every extreme that they name: Clips are consecutive runs of frames: clip_start never falls, clip_start[t] <= t, clip_start[t] == t at each clip's first frame; every clip has 9 to 33 frames except the last two, which are cut by the bin's end; the bin's last frame begins a clip of its own.
All inputs are finite; a program needn't handle non-finite values.
Results may differ from the reference program's by a relative error of at most 0.012.
Values may be sent and summed in bfloat16 or wider, within the bound.
A program may use at most 128 MiB of HBM per device.

```python
import jax
import jax.numpy as jnp
from jax import lax

C = 512
CL = 16
D = 3072
PATCH_EDGE = 4
TAPS = 3
CLIP_MIN = 9
CLIP_MAX = 33
PIX = 2048
FRAMES = 32
TOKENS = 16384
N_TM = 8
N_SEQ = 4


def draw_clip_start(key, part):
    clip_count = FRAMES // CLIP_MIN + 1
    lengths = jax.random.randint(jax.random.fold_in(key, 17), (clip_count,), CLIP_MIN, CLIP_MAX + 1).astype(jnp.int32)
    clip_ends = jnp.cumsum(lengths).astype(jnp.int32)
    clip_first = clip_ends - lengths
    frame_order = jnp.arange(FRAMES, dtype=jnp.int32)
    owner_clip = jnp.sum((clip_ends[None, :] <= frame_order[:, None]).astype(jnp.int32), axis=1)
    clip_index = jnp.arange(clip_count, dtype=jnp.int32)
    picked = jnp.where(clip_index[None, :] == owner_clip[:, None], clip_first[None, :], 0)
    starts = jnp.sum(picked, axis=1).astype(jnp.int32)
    return jnp.where(frame_order == FRAMES - 1, frame_order, starts).astype(jnp.int32)


def strengthened(drawn, rng, source, target, shards_of, factor):
    owner, partner = [(jnp.arange(drawn.shape[dim]) // (drawn.shape[dim] // shards_of)).reshape([-1 if axis == dim else 1 for axis in range(drawn.ndim)]) for dim in (source, target)]
    chosen = jax.random.permutation(rng, shards_of)[partner]
    strong = (owner == chosen) | (owner == (partner + shards_of // 2) % shards_of)
    return jnp.where(strong, factor * drawn, drawn)


def shard_levels(own_key, extent, split, low, high):
    level = 1.0
    for dim, shards_of in split:
        heights = jax.random.uniform(jax.random.fold_in(jax.random.fold_in(own_key, 6), dim), (shards_of,), jnp.float32, low / len(split), high / len(split))
        level = level * jnp.repeat(jnp.exp(heights), extent[dim] // shards_of).reshape((-1,) + (1,) * (len(extent) - 1 - dim))
    return level


def scatter_about(own_key, shape, width, reach, pieces=(), held_as=jnp.bfloat16):
    values = jax.random.normal(own_key, shape, jnp.float32) * width
    if len(pieces) > 0:
        values = shard_levels(own_key, shape, pieces, -0.22, 0.18) * values
    return jnp.clip(values, min=-reach, max=reach).astype(held_as)


def noise_with(stream_key, dims, scale, most, pieces, heavy, kind=jnp.bfloat16):
    values = scale * jax.random.normal(stream_key, dims, jnp.float32)
    if pieces:
        values = values * shard_levels(stream_key, dims, pieces, -0.22, 0.18)
    return jnp.clip(strengthened(values, jax.random.fold_in(stream_key, 3), *heavy), -most, most).astype(kind)


def setup_inputs(seed: int = 0) -> dict:
    keys = jax.random.split(jax.random.key(seed), 10)
    latents = scatter_about(keys[0], (FRAMES, CL, PIX), 1.0, 6.0, ((0, 8), (2, 4)))
    hidden = scatter_about(keys[1], (TOKENS, D), 1.0, 6.0, ((0, 32),))
    grad_out = noise_with(keys[2], (FRAMES, C, PIX), 1.0, 6.0, ((0, 8), (2, 4)), (0, 1, 8, 2.0))
    conv_in_w = scatter_about(keys[3], (TAPS, C, CL), (TAPS * CL) ** -0.5, 0.875)
    conv_in_b = scatter_about(keys[4], (C,), 1.0, 4.0, (), jnp.float32)
    conv_w = scatter_about(keys[5], (TAPS, C, C), (TAPS * C) ** -0.5, 0.15625)
    final_w = scatter_about(keys[6], (D, CL * PATCH_EDGE), D ** -0.5, 0.109375)
    modulation = scatter_about(keys[7], (2, D), 0.5, 3.0, (), jnp.float32)
    clip_start = draw_clip_start(jax.random.fold_in(keys[9], 71), 0)
    return dict(latents=latents, hidden=hidden, grad_out=grad_out, conv_in_w=conv_in_w, conv_in_b=conv_in_b, conv_w=conv_w, final_w=final_w, modulation=modulation, clip_start=clip_start)


def silu_parts(pre_act):
    sigmoid_v = jax.nn.sigmoid(pre_act)
    return (pre_act * sigmoid_v, sigmoid_v * (1.0 + pre_act * (1.0 - sigmoid_v)))

def reference(latents, hidden, grad_out, conv_in_w, conv_in_b, conv_w, final_w, modulation, clip_start):
    frames = latents.shape[0]
    chans = grad_out.shape[1]
    latent_channels = latents.shape[1]
    frame_order = jnp.arange(frames, dtype=jnp.int32)
    source = [jnp.maximum(frame_order - offset, clip_start).astype(jnp.int32) for offset in range(TAPS)]
    blocks = N_SEQ
    block_width = PIX // blocks

    def to_blocks(array):
        return array.reshape(array.shape[0], array.shape[1], blocks, block_width).transpose(2, 0, 1, 3)
    w_in = conv_in_w.astype(jnp.float32)
    w_mid = conv_w.astype(jnp.float32)

    def decode_block(running_totals, piece_list):
        lat_block, grad_block = piece_list
        lat_f = lat_block.astype(jnp.float32)
        grad_f = grad_block.astype(jnp.float32)
        pre_act = conv_in_b[None, :, None] + sum((jnp.einsum('oc,tcp->top', w_in[offset], lat_f[source[offset]]) for offset in range(TAPS)))
        activation, silu_slope = silu_parts(pre_act)
        act_low = lax.optimization_barrier(activation.astype(jnp.bfloat16))
        act_f = act_low.astype(jnp.float32)
        grad_act = sum((jnp.zeros((frames, chans, block_width), jnp.float32).at[source[offset]].add(jnp.einsum('oi,top->tip', w_mid[offset], grad_f)) for offset in range(TAPS)))
        grad_pre = lax.optimization_barrier((grad_act * silu_slope).astype(jnp.bfloat16))
        pre_f = grad_pre.astype(jnp.float32)
        lat_grad = sum((jnp.zeros((frames, latent_channels, block_width), jnp.float32).at[source[offset]].add(jnp.einsum('oc,top->tcp', w_in[offset], pre_f)) for offset in range(TAPS)))
        conv_term = jnp.stack([jnp.einsum('top,tip->oi', grad_f, act_f[source[offset]]) for offset in range(TAPS)], axis=1)
        in_term = jnp.stack([jnp.einsum('top,tcp->oc', pre_f, lat_f[source[offset]]) for offset in range(TAPS)], axis=0)
        bias_term = lax.optimization_barrier(jnp.sum(pre_f, axis=(0, 2)))
        new_totals = (running_totals[0] + conv_term, running_totals[1] + in_term, running_totals[2] + bias_term)
        return (new_totals, lat_grad.astype(jnp.bfloat16))
    start_totals = (jnp.zeros((chans, TAPS, chans), jnp.float32), jnp.zeros((TAPS, chans, latent_channels), jnp.float32), jnp.zeros((chans,), jnp.float32))
    running_totals, grad_blocks = lax.scan(decode_block, start_totals, (to_blocks(latents), to_blocks(grad_out)))
    convolution_weight_gradient, input_convolution_gradient, input_bias_gradient = running_totals
    latent_grad = grad_blocks.transpose(1, 2, 0, 3).reshape(frames, latent_channels, PIX)
    token_gradient = latent_grad.reshape(frames, latent_channels, PIX // PATCH_EDGE, PATCH_EDGE).transpose(0, 2, 1, 3).reshape(frames * (PIX // PATCH_EDGE), latent_channels * PATCH_EDGE)
    group_list = N_TM * N_SEQ
    rows_per_block = hidden.shape[0] // group_list
    shift_vec = modulation[0]
    scale_vec = modulation[1]

    def transformer_block(running_totals, piece_list):
        hid_block, grad_block = piece_list
        hid_f = hid_block.astype(jnp.float32)
        center = hid_f - lax.optimization_barrier(jnp.mean(hid_f, axis=1, keepdims=True))
        variance = lax.optimization_barrier(jnp.mean(center * center, axis=1, keepdims=True))
        inv_std = lax.rsqrt(variance + 1e-06)
        normed = center * inv_std
        modulated = (normed * (1.0 + scale_vec) + shift_vec).astype(jnp.bfloat16)
        final_term = jnp.dot(modulated.T, grad_block, preferred_element_type=jnp.float32)
        mod_in = jnp.dot(grad_block, final_w.T, preferred_element_type=jnp.float32)
        mod_term = jnp.stack([lax.optimization_barrier(jnp.sum(mod_in, axis=0)), lax.optimization_barrier(jnp.sum(mod_in * normed, axis=0))])
        norm_grad = mod_in * (1.0 + scale_vec)
        hid_grad = inv_std * (norm_grad - lax.optimization_barrier(jnp.mean(norm_grad, axis=1, keepdims=True)) - normed * lax.optimization_barrier(jnp.mean(norm_grad * normed, axis=1, keepdims=True)))
        return ((running_totals[0] + final_term, running_totals[1] + mod_term), hid_grad.astype(jnp.bfloat16))
    transformer_start = (jnp.zeros((hidden.shape[1], latent_channels * PATCH_EDGE), jnp.float32), jnp.zeros((2, hidden.shape[1]), jnp.float32))
    transformer_totals, hidden_blocks = lax.scan(transformer_block, transformer_start, (hidden.reshape(group_list, rows_per_block, hidden.shape[1]), token_gradient.reshape(group_list, rows_per_block, latent_channels * PATCH_EDGE)))
    hidden_input_gradient = hidden_blocks.reshape(hidden.shape[0], hidden.shape[1])
    return (hidden_input_gradient, convolution_weight_gradient, input_convolution_gradient, input_bias_gradient, transformer_totals[0], transformer_totals[1])
```

```python
import functools

import jax
import jax.numpy as jnp
from jax import lax
from jax.experimental import pallas as pl
from jax.experimental.pallas import tpu as pltpu
from jax.sharding import PartitionSpec as P

F32 = jnp.float32
BF16 = jnp.bfloat16
MESH = pl.DeviceIdType.MESH
PATCH = 4
CORES = 2
TAPS = 3
HALO = 4
MAIN_VMEM = 44 * 1024 * 1024
SMALL_VMEM = 12 * 1024 * 1024


def dot(a, b, ca, cb):
    return lax.dot_general(a, b, (((ca,), (cb,)), ((), ())), preferred_element_type=F32)


def load_in_weights(w_in_ref, b_ref, w64):
    bias = b_ref[...]
    hi = bias.astype(BF16)
    mid = (bias - hi.astype(F32)).astype(BF16)
    lo = (bias - hi.astype(F32) - mid.astype(F32)).astype(BF16)
    pad = jnp.zeros((16 - 3, bias.shape[1]), F32)
    rows = jnp.concatenate(
        [w_in_ref[...].astype(F32), hi.astype(F32), mid.astype(F32), lo.astype(F32), pad], axis=0
    )
    w64[...] = rows.T.astype(BF16)


def sigmoid(x):
    return 0.5 * jnp.tanh(0.5 * x) + 0.5


def main_kernel(
    n_tm, n_seq,
    clip_ref, lat_hbm, hid_hbm, grad_hbm, w_in_ref, b_ref, w_hbm, fw_ref, modu_ref,
    dx_ref, wg_ref, gath,
    latx, g, wraw, hid, nb, inv, w64, z, tab, act, slope, ga, gp_parts, misc, lg, lgh, lgh_in, lgs, tok,
    acc, w4, wcore, whalf, wrecv, wsum, wrecv2,
    tgs, tcol, facc, macc, f4, fcore, fhalf, frecv, fsum, frecv2,
    s_in, s_lat, r_lat, s_halo, r_halo, s_tok, r_tok,
    s_wc, r_wc, s_w, r_w, s_w2, r_w2,
    s_fc, r_fc, s_f, r_f, s_f2, r_f2, s_g, r_g, s_g2, r_g2, s_gc, r_gc,
):
    i = lax.axis_index("tm")
    j = lax.axis_index("seq")
    chips = n_tm // CORES
    core = lax.rem(i, CORES)
    chip = lax.div(i, CORES)
    other = CORES - 1 - core
    sibling = (chip * CORES + other, j)
    tms = [(d, lax.rem(chip + d, chips)) for d in range(1, chips)]
    seqs = [(d, lax.rem(j + d, n_seq)) for d in range(1, n_seq)]
    slab, chans = g.shape[:2]
    cl, width = latx.shape[1:]
    frames = clip_ref.shape[0]
    d_model = hid.shape[1]
    first = i * slab

    own_lat = pltpu.make_async_copy(lat_hbm, latx.at[pl.ds(HALO, slab)], s_in.at[0])
    own_w = pltpu.make_async_copy(w_hbm, wraw, s_in.at[1])
    own_g = pltpu.make_async_copy(grad_hbm, g, s_in.at[2])
    own_hid = pltpu.make_async_copy(hid_hbm, hid, s_in.at[3])
    for c in (own_lat, own_w, own_g, own_hid):
        c.start()

    barrier = pltpu.get_barrier_semaphore()
    for _, p in tms:
        pl.semaphore_signal(barrier, inc=1, device_id=(p * CORES + core, j), device_id_type=MESH)
    pl.semaphore_signal(barrier, inc=1, device_id=sibling, device_id_type=MESH)
    for _, p in seqs:
        pl.semaphore_signal(barrier, inc=1, device_id=(i, p), device_id_type=MESH)
    for step in (1, n_tm - 1):
        pl.semaphore_signal(barrier, inc=1, device_id=(lax.rem(i + step, n_tm), j), device_id_type=MESH)

    def copy(src, dst, send, recv, to):
        return pltpu.make_async_remote_copy(
            src_ref=src, dst_ref=dst, send_sem=send, recv_sem=recv, device_id=to, device_id_type=MESH
        )

    load_in_weights(w_in_ref, b_ref, w64)
    own_lat.wait()
    pl.semaphore_wait(barrier, chips + n_seq + 1)

    def lat_copy(to):
        return copy(latx.at[pl.ds(slab, HALO)], latx.at[pl.ds(0, HALO)], s_lat, r_lat, (to, j))

    @pl.when(i < n_tm - 1)
    def _():
        lat_copy(i + 1).start()

    @pl.when(i == 0)
    def _():
        latx[0:HALO] = jnp.zeros_like(latx[0:HALO])

    own_w.wait()
    taps_t = [wraw[tap].T for tap in range(TAPS)]
    for tap in range(TAPS):
        tab[tap] = taps_t[tap]
    later = taps_t[1].astype(F32) + taps_t[2].astype(F32)
    tab[3] = later.astype(BF16)
    tab[4] = (later + taps_t[0].astype(F32)).astype(BF16)
    tab[5] = jnp.zeros_like(tab[5])

    @pl.when(i < n_tm - 1)
    def _():
        lat_copy(i + 1).wait_send()

    @pl.when(i > 0)
    def _():
        lat_copy(i).wait_recv()

    def clip_of(frame):
        return clip_ref[jnp.clip(frame, 0, frames - 1)]

    def source(frame, tap):
        return jnp.maximum(frame - tap, clip_of(frame))

    @pl.loop(0, slab + 2)
    def _(r):
        frame = first + r - 2
        for tap in range(TAPS):
            row = jnp.clip(source(frame, tap) - first + HALO, 0, slab + HALO - 1)
            z[r, tap * cl : (tap + 1) * cl] = latx[row]
        z[r, TAPS * cl :] = jnp.ones((cl, width), BF16)
        pre = dot(w64[...], z[r], 1, 0)
        sig = sigmoid(pre)
        a = pre * sig
        act[r] = a.astype(BF16)
        slope[r] = sig + a * (1.0 - sig)

    misc[...] = jnp.zeros_like(misc)
    ga[0:2] = jnp.zeros_like(ga[0:2])
    own_g.wait()

    def finish(r, total):
        grad_pre = (total * slope[r]).astype(BF16)
        misc[...] += dot(z[r], grad_pre, 1, 1)
        gp_parts[r] = dot(w_in_ref[...], grad_pre, 1, 0)

    @pl.loop(0, slab)
    def _(t):
        frame = first + t
        start = clip_of(frame)
        back1 = start < frame
        back2 = start < frame - 1
        at0 = jnp.where(back1, 0, 4)
        at1 = jnp.where(back2, 1, jnp.where(back1, 3, 5))
        at2 = jnp.where(back2, 2, 5)
        grad = g[t]
        ga[t + 2] = dot(tab[at0], grad, 1, 0)
        ga[t + 1] += dot(tab[at1], grad, 1, 0)
        finish(t, ga[t] + dot(tab[at2], grad, 1, 0))

    @pl.loop(slab, slab + 2)
    def _(r):
        finish(r, ga[r])

    lg[...] = jnp.zeros_like(lg)
    for r in range(slab + 2):
        frame = first + r - 2
        start = clip_of(frame)
        back1 = jnp.where(start < frame, 1.0, 0.0).astype(F32)
        back2 = jnp.where(start < frame - 1, 1.0, 0.0).astype(F32)
        p0, p1, p2 = [gp_parts[r, tap * cl : (tap + 1) * cl] for tap in range(TAPS)]
        lg[r + 2] += p0 + (1.0 - back1) * (p1 + p2)
        lg[r + 1] += back1 * p1 + (back1 - back2) * p2
        lg[r] += back2 * p2

    lgh[...] = lg[0:HALO].astype(BF16)

    def halo_copy(to):
        return copy(lgh, lgh_in, s_halo, r_halo, (to, j))

    @pl.when(i > 0)
    def _():
        halo_copy(i - 1).start()

    @pl.when(i == n_tm - 1)
    def _():
        lgh_in[...] = jnp.zeros_like(lgh_in)

    rows = chans // (n_tm * n_seq)
    block = n_seq * rows

    def weight(tap):
        @pl.loop(0, slab)
        def _(t):
            row = jnp.clip(source(first + t, tap) - first + 2, 0, slab + 1)
            part = dot(g[t], act[row], 1, 1)

            @pl.when(t == 0)
            def _():
                acc[...] = part

            @pl.when(t > 0)
            def _():
                acc[...] += part

        for q in range(chips):
            for c in range(CORES):
                at = (q * CORES + c) * block
                w4[tap, c, q] = acc[at : at + block].astype(BF16)

    w_core = [
        copy(w4.at[tap, other], wcore.at[tap], s_wc.at[tap], r_wc.at[tap], sibling) for tap in range(TAPS)
    ]
    w_xy = [
        [
            copy(whalf.at[tap, p], wrecv.at[tap, d - 1], s_w.at[tap, d - 1], r_w.at[tap, d - 1], (p * CORES + core, j))
            for d, p in tms
        ]
        for tap in range(TAPS)
    ]
    w_z = [
        [
            copy(wsum.at[tap, p], wrecv2.at[tap, d - 1], s_w2.at[tap, d - 1], r_w2.at[tap, d - 1], (i, p))
            for d, p in seqs
        ]
        for tap in range(TAPS)
    ]

    def weight_xy(tap):
        w_core[tap].wait()
        whalf[tap] = (w4[tap, core].astype(F32) + wcore[tap].astype(F32)).astype(BF16)
        for c in w_xy[tap]:
            c.start()

    def weight_z(tap):
        for c in w_xy[tap]:
            c.wait()
        total = whalf[tap, chip].astype(F32)
        for k in range(chips - 1):
            total = total + wrecv[tap, k].astype(F32)
        for p in range(n_seq):
            wsum[tap, p] = total[p * rows : (p + 1) * rows].astype(BF16)
        for c in w_z[tap]:
            c.start()

    def weight_end(tap):
        for c in w_z[tap]:
            c.wait()
        total = wsum[tap, j].astype(F32)
        for k in range(n_seq - 1):
            total = total + wrecv2[tap, k].astype(F32)
        wg_ref[tap] = total

    weight(0)
    w_core[0].start()

    @pl.when(i > 0)
    def _():
        halo_copy(i - 1).wait_send()

    @pl.when(i < n_tm - 1)
    def _():
        halo_copy(i).wait_recv()

    lgs[...] = (lg[HALO : HALO + slab] + lgh_in[...].astype(F32)).astype(BF16)
    tok_copies = [copy(lgs.at[p], tok.at[j], s_tok.at[d - 1], r_tok.at[d - 1], (i, p)) for d, p in seqs]
    for c in tok_copies:
        c.start()

    weight(1)
    w_core[1].start()
    weight_xy(0)
    weight(2)
    w_core[2].start()
    weight_xy(1)

    own_hid.wait()
    step_rows = 32

    @pl.loop(0, hid.shape[0] // step_rows)
    def _(r):
        at = pl.ds(pl.multiple_of(r * step_rows, step_rows), step_rows)
        h = hid[at, :].astype(F32)
        center = h - jnp.mean(h, axis=1, keepdims=True)
        scaled = lax.rsqrt(jnp.mean(center * center, axis=1, keepdims=True) + 1e-06)
        nb[at, :] = (center * scaled).astype(BF16)
        inv[at, :] = jnp.broadcast_to(scaled, (step_rows, inv.shape[1]))

    weight_xy(2)

    n = width // PATCH
    row = lax.broadcasted_iota(jnp.int32, (width, width), 0)
    col = lax.broadcasted_iota(jnp.int32, (width, width), 1)
    spread = jnp.where(row == lax.rem(col, n) * PATCH + lax.div(col, n), 1.0, 0.0).astype(BF16)
    e = cl * PATCH
    row = lax.broadcasted_iota(jnp.int32, (e, e), 0)
    col = lax.broadcasted_iota(jnp.int32, (e, e), 1)
    order = jnp.where(row == lax.rem(col, cl) * PATCH + lax.div(col, cl), 1.0, 0.0).astype(BF16)
    facc[...] = jnp.zeros_like(facc)
    tcol[...] = jnp.zeros_like(tcol)
    shift = modu_ref[0:1, :]
    scale = 1.0 + modu_ref[1:2, :]

    for c in tok_copies:
        c.wait()
    tok[j] = lgs[j]

    def rows_of(r):
        return pl.ds(pl.multiple_of(r * n, n), n)

    @pl.loop(0, n_seq)
    def _(r):
        split = dot(tok[r], spread, 1, 0)
        stack = jnp.concatenate([split[:, q * n : (q + 1) * n] for q in range(PATCH)], axis=0)
        tg_t = dot(order, stack.astype(BF16), 1, 0)
        tgs[rows_of(r), :] = tg_t.T.astype(BF16)
        facc[...] += dot(tg_t.astype(BF16), nb[rows_of(r), :], 1, 0)
        tcol[...] += jnp.broadcast_to(jnp.sum(tg_t, axis=1, keepdims=True), tcol.shape)

    column = tcol[:, 0:1]
    fw = fw_ref[...].astype(F32)
    macc[0:1] = jnp.sum(fw * column, axis=0, keepdims=True)
    macc[1:2] = jnp.sum(fw * facc[...], axis=0, keepdims=True)
    facc[...] = facc[...] * scale + column * shift

    wf = d_model // n_tm
    wm = chans // n_tm
    er = e // n_seq
    pieces = d_model // chans
    small = jnp.concatenate(
        [misc[0 : TAPS * cl + 1, :]]
        + [macc[b : b + 1, p * chans : (p + 1) * chans] for b in range(2) for p in range(pieces)]
        + [jnp.zeros((e - TAPS * cl - 1 - 2 * pieces, chans), F32)],
        axis=0,
    )
    for a in range(n_tm):
        for b in range(n_seq):
            f4[a % CORES, a // CORES, b, :, :wf] = facc[b * er : (b + 1) * er, a * wf : (a + 1) * wf].astype(BF16)
            f4[a % CORES, a // CORES, b, :, wf : wf + wm] = small[b * er : (b + 1) * er, a * wm : (a + 1) * wm].astype(BF16)
            if wf + wm < f4.shape[4]:
                f4[a % CORES, a // CORES, b, :, wf + wm :] = jnp.zeros((er, f4.shape[4] - wf - wm), BF16)
    f_core = copy(f4.at[other], fcore, s_fc, r_fc, sibling)
    f_core.start()

    def input_gradient(r):
        normed = nb[rows_of(r), :].astype(F32)
        ng = dot(tgs[rows_of(r), :], fw_ref[...], 1, 0) * scale
        m1 = jnp.mean(ng, axis=1, keepdims=True)
        m2 = jnp.mean(ng * normed, axis=1, keepdims=True)
        dx_ref[rows_of(r), :] = (inv[rows_of(r), 0:1] * (ng - m1 - normed * m2)).astype(BF16)

    pl.loop(0, n_seq // 2)(input_gradient)
    f_core.wait()
    for q in range(chips):
        fhalf[q] = (f4[core, q].astype(F32) + fcore[q].astype(F32)).astype(BF16)
    f_copies = [
        copy(fhalf.at[p], frecv.at[d - 1], s_f.at[d - 1], r_f.at[d - 1], (p * CORES + core, j))
        for d, p in tms
    ]
    for c in f_copies:
        c.start()
    pl.loop(n_seq // 2, n_seq)(input_gradient)
    weight_z(0)
    weight_z(1)
    for c in f_copies:
        c.wait()
    total = fhalf[chip].astype(F32)
    for k in range(chips - 1):
        total = total + frecv[k].astype(F32)
    fsum[...] = total.astype(BF16)
    f2_copies = [
        copy(fsum.at[p], frecv2.at[d - 1], s_f2.at[d - 1], r_f2.at[d - 1], (i, p)) for d, p in seqs
    ]
    for c in f2_copies:
        c.start()
    weight_z(2)
    for c in f2_copies:
        c.wait()
    total = fsum[j].astype(F32)
    for k in range(n_seq - 1):
        total = total + frecv2[k].astype(F32)
    gath[core, chip, j] = total.astype(BF16)
    g_copies = [
        copy(gath.at[core, chip, j], gath.at[core, chip, j], s_g.at[d - 1], r_g.at[d - 1], (i, p)) for d, p in seqs
    ]
    for c in g_copies:
        c.start()
    weight_end(0)
    weight_end(1)
    for c in g_copies:
        c.wait()
    g2_copies = [
        copy(gath.at[core, chip], gath.at[core, chip], s_g2.at[d - 1], r_g2.at[d - 1], (p * CORES + core, j))
        for d, p in tms
    ]
    for c in g2_copies:
        c.start()
    weight_end(2)
    for c in g2_copies:
        c.wait()
    g_core = copy(gath.at[core], gath.at[core], s_gc, r_gc, sibling)
    g_core.start()
    g_core.wait()


def unpack_kernel(gath, wg_ref, dx_in, fin_ref, mod_ref, in_ref, bias_ref, wg_out, dx_hbm, small, sem):
    dx_copy = pltpu.make_async_copy(dx_in, dx_hbm, sem)
    dx_copy.start()
    cores, chips, n_seq, er, _ = gath.shape
    n_tm = cores * chips
    d_model = fin_ref.shape[1]
    taps_cl, chans = in_ref.shape
    wf = d_model // n_tm
    wm = chans // n_tm
    pieces = d_model // chans
    for a in range(n_tm):
        for b in range(n_seq):
            fin_ref[b * er : (b + 1) * er, a * wf : (a + 1) * wf] = gath[a % cores, a // cores, b, :, :wf].astype(F32)
            small[b * er : (b + 1) * er, a * wm : (a + 1) * wm] = gath[a % cores, a // cores, b, :, wf : wf + wm].astype(F32)
    in_ref[...] = small[:taps_cl, :]
    bias_ref[...] = small[taps_cl : taps_cl + 1, :]
    for b in range(2):
        for p in range(pieces):
            at = taps_cl + 1 + b * pieces + p
            mod_ref[b : b + 1, p * chans : (p + 1) * chans] = small[at : at + 1, :]
    wg_out[...] = wg_ref[...]
    dx_copy.wait()


def local(n_tm, n_seq, latents, hidden, grad_out, conv_in_w, conv_in_b, conv_w, final_w, modulation, clip_start):
    slab, cl, width = latents.shape
    taps, chans = conv_w.shape[:2]
    tokens, d_model = hidden.shape
    rows = chans // (n_tm * n_seq)
    block = n_seq * rows
    chips = n_tm // CORES
    w_in = conv_in_w.transpose(0, 2, 1).reshape(taps * cl, chans)
    bias = conv_in_b.reshape(1, chans)
    e = cl * PATCH
    er = e // n_seq
    cw = -(-((d_model + chans) // n_tm) // 128) * 128
    vmem = pl.BlockSpec(memory_space=pltpu.VMEM)
    hbm = pl.BlockSpec(memory_space=pltpu.HBM)
    smem = pl.BlockSpec(memory_space=pltpu.SMEM)
    dma = pltpu.SemaphoreType.DMA
    nt, ns = chips - 1, n_seq - 1

    def b16(*shape):
        return pltpu.VMEM(shape, BF16)

    def f32(*shape):
        return pltpu.VMEM(shape, F32)

    dx, wg, gath = pl.pallas_call(
        functools.partial(main_kernel, n_tm, n_seq),
        out_shape=(
            jax.ShapeDtypeStruct((tokens, d_model), BF16),
            jax.ShapeDtypeStruct((taps, rows, chans), F32),
            jax.ShapeDtypeStruct((CORES, chips, n_seq, er, cw), BF16),
        ),
        in_specs=[smem, hbm, hbm, hbm, vmem, vmem, hbm, vmem, vmem],
        out_specs=(vmem, vmem, vmem),
        scratch_shapes=[
            b16(slab + HALO, cl, width),
            b16(slab, chans, width),
            b16(taps, chans, chans),
            b16(tokens, d_model),
            b16(tokens, d_model),
            f32(tokens, 128),
            b16(chans, 4 * cl),
            b16(slab + 2, 4 * cl, width),
            b16(taps + 3, chans, chans),
            b16(slab + 2, chans, width),
            f32(slab + 2, chans, width),
            f32(slab + 2, chans, width),
            f32(slab + 2, taps * cl, width),
            f32(4 * cl, chans),
            f32(slab + HALO, cl, width),
            b16(HALO, cl, width),
            b16(HALO, cl, width),
            b16(slab, cl, width),
            b16(n_seq, cl, width),
            f32(chans, chans),
            b16(taps, CORES, chips, block, chans),
            b16(taps, chips, block, chans),
            b16(taps, chips, block, chans),
            b16(taps, nt, block, chans),
            b16(taps, n_seq, rows, chans),
            b16(taps, ns, rows, chans),
            b16(tokens, e),
            f32(e, 128),
            f32(e, d_model),
            f32(8, d_model),
            b16(CORES, chips, n_seq, er, cw),
            b16(chips, n_seq, er, cw),
            b16(chips, n_seq, er, cw),
            b16(nt, n_seq, er, cw),
            b16(n_seq, er, cw),
            b16(ns, er, cw),
            dma((4,)), dma(()), dma(()), dma(()), dma(()), dma((ns,)), dma((ns,)),
            dma((taps,)), dma((taps,)), dma((taps, nt)), dma((taps, nt)), dma((taps, ns)), dma((taps, ns)),
            dma(()), dma(()), dma((nt,)), dma((nt,)), dma((ns,)), dma((ns,)),
            dma((ns,)), dma((ns,)), dma((nt,)), dma((nt,)), dma(()), dma(()),
        ],
        compiler_params=pltpu.CompilerParams(
            vmem_limit_bytes=MAIN_VMEM, collective_id=0, has_side_effects=True
        ),
        name="main",
    )(clip_start, latents, hidden, grad_out, w_in, bias, conv_w, final_w.T, modulation)
    fin, mod, w_in_grad, bias_grad, wg, dx = pl.pallas_call(
        unpack_kernel,
        out_shape=(
            jax.ShapeDtypeStruct((e, d_model), F32),
            jax.ShapeDtypeStruct((2, d_model), F32),
            jax.ShapeDtypeStruct((taps * cl, chans), F32),
            jax.ShapeDtypeStruct((1, chans), F32),
            jax.ShapeDtypeStruct((taps, rows, chans), F32),
            jax.ShapeDtypeStruct((tokens, d_model), BF16),
        ),
        in_specs=[vmem, vmem, pl.BlockSpec(memory_space=pl.ANY)],
        out_specs=(vmem,) * 5 + (hbm,),
        scratch_shapes=[pltpu.VMEM((e, chans), F32), dma(())],
        compiler_params=pltpu.CompilerParams(vmem_limit_bytes=SMALL_VMEM),
        name="unpack",
    )(gath, wg, dx)
    return (
        dx,
        wg.transpose(1, 0, 2),
        w_in_grad.reshape(taps, cl, chans).transpose(0, 2, 1),
        bias_grad.reshape(chans),
        fin.T,
        mod,
    )


def solution(mesh):
    return jax.shard_map(
        functools.partial(local, mesh.shape["tm"], mesh.shape["seq"]),
        mesh=mesh,
        in_specs=(
            P("tm", None, "seq"),
            P(("tm", "seq"), None),
            P("tm", None, "seq"),
            P(),
            P(),
            P(),
            P(),
            P(),
            P(),
        ),
        out_specs=(P(("tm", "seq"), None), P(("tm", "seq"), None, None), P(), P(), P(), P()),
        check_vma=False,
    )
```

```python
import functools

import jax
import jax.numpy as jnp
from jax import lax
from jax.experimental import pallas as pl
from jax.experimental.pallas import tpu as pltpu
from jax.sharding import PartitionSpec as P

F32 = jnp.float32
BF16 = jnp.bfloat16
MESH = pl.DeviceIdType.MESH
PATCH = 4
CORES = 2
TAPS = 3
HALO = 4
MAIN_VMEM = 46 * 1024 * 1024
SMALL_VMEM = 12 * 1024 * 1024


def dot(a, b, ca, cb):
    return lax.dot_general(a, b, (((ca,), (cb,)), ((), ())), preferred_element_type=F32)


def load_in_weights(w_in_ref, b_ref, w64):
    bias = b_ref[...]
    hi = bias.astype(BF16)
    mid = (bias - hi.astype(F32)).astype(BF16)
    lo = (bias - hi.astype(F32) - mid.astype(F32)).astype(BF16)
    pad = jnp.zeros((16 - 3, bias.shape[1]), F32)
    rows = jnp.concatenate(
        [w_in_ref[...].astype(F32), hi.astype(F32), mid.astype(F32), lo.astype(F32), pad], axis=0
    )
    w64[...] = rows.T.astype(BF16)


def sigmoid(x):
    return 0.5 * jnp.tanh(0.5 * x) + 0.5


def main_kernel(
    n_tm, n_seq,
    clip_hbm, lat_hbm, hid_hbm, grad_hbm, w_in_hbm, b_hbm, w_hbm, fw_hbm, modu_hbm,
    dx_ref, wg_ref, gath,
    clip_ref, w_in_ref, b_ref, fw_ref, modu_ref,
    latx, g, hid, nb, inv, w64, z, tab, act, ga, gp, parts, misc, lg, lgh, lgs, tok, tokh,
    w4, wcore, whalf, wrecv, wsum, wrecv2,
    spread, tgs, facc, macc, f4, fcore, fhalf, frecv, fsum, frecv2,
    s_in, s_g_in, s_lat, r_lat, s_halo, r_halo, s_tok, r_tok,
    s_wc, r_wc, s_w, r_w, s_w2, r_w2,
    s_fc, r_fc, s_f, r_f, s_f2, r_f2, s_g, r_g, s_g2, r_g2, s_gc, r_gc,
):
    i = lax.axis_index("tm")
    j = lax.axis_index("seq")
    chips = n_tm // CORES
    core = lax.rem(i, CORES)
    chip = lax.div(i, CORES)
    other = CORES - 1 - core
    sibling = (chip * CORES + other, j)
    tms = [(d, lax.rem(chip + d, chips)) for d in range(1, chips)]
    seqs = [(d, lax.rem(j + d, n_seq)) for d in range(1, n_seq)]
    slab, chans = g.shape[:2]
    cl, width = latx.shape[1:]
    frames = clip_ref.shape[0]
    d_model = hid.shape[1]
    first = i * slab

    loads = [
        pltpu.make_async_copy(src, dst, s_in.at[k])
        for k, (src, dst) in enumerate(
            [
                (clip_hbm, clip_ref),
                (w_hbm, tab.at[pl.ds(0, TAPS)]),
                (w_in_hbm, w_in_ref),
                (b_hbm, b_ref),
                (lat_hbm, latx.at[pl.ds(HALO, slab)]),
                (hid_hbm, hid),
                (fw_hbm, fw_ref),
                (modu_hbm, modu_ref),
            ]
        )
    ]
    own_clip, own_w, own_w_in, own_b, own_lat, own_hid, own_fw, own_modu = loads
    own_g = [pltpu.make_async_copy(grad_hbm.at[t], g.at[t], s_g_in.at[t]) for t in range(slab)]
    for c in [own_clip, own_w] + own_g + [own_w_in, own_b, own_lat, own_fw, own_modu, own_hid]:
        c.start()

    barrier = pltpu.get_barrier_semaphore()
    greeted = [(p * CORES + core, j) for _, p in tms] + [sibling] + [(i, p) for _, p in seqs]
    greeted += [(lax.rem(i + 1, n_tm), p) for p in range(n_seq)] + [(lax.rem(i + n_tm - 1, n_tm), j)]
    for to in greeted:
        pl.semaphore_signal(barrier, inc=1, device_id=to, device_id_type=MESH)

    def copy(src, dst, send, recv, to):
        return pltpu.make_async_remote_copy(
            src_ref=src, dst_ref=dst, send_sem=send, recv_sem=recv, device_id=to, device_id_type=MESH
        )

    def lat_copy(to):
        return copy(lat_hbm.at[pl.ds(slab - HALO, HALO)], latx.at[pl.ds(0, HALO)], s_lat, r_lat, (to, j))

    def clip_of(frame):
        return clip_ref[jnp.clip(frame, 0, frames - 1)]

    def source(frame, tap):
        return jnp.maximum(frame - tap, clip_of(frame))

    own_clip.wait()
    own_w.wait()
    later = tab[1].astype(F32) + tab[2].astype(F32)
    tab[TAPS] = later.astype(BF16)
    tab[TAPS + 1] = (later + tab[0].astype(F32)).astype(BF16)
    tab[TAPS + 2] = jnp.zeros_like(tab[TAPS + 2])

    def choice(t, back):
        start = clip_of(first + t)
        back1 = start < first + t
        back2 = start < first + t - 1
        if back == 0:
            return jnp.where(back1, 0, TAPS + 1)
        if back == 1:
            return jnp.where(back2, 1, jnp.where(back1, TAPS, TAPS + 2))
        return jnp.where(back2, 2, TAPS + 2)

    def grad_act(r):
        ga[r] = sum(
            dot(tab[choice(r - 2 + back, back)], g[r - 2 + back], 0, 0)
            for back in range(TAPS)
            if 0 <= r - 2 + back < slab
        )

    own_g[0].wait()
    grad_act(0)
    own_g[1].wait()
    grad_act(1)
    pl.semaphore_wait(barrier, len(greeted))

    @pl.when(i < n_tm - 1)
    def _():
        lat_copy(i + 1).start()

    @pl.when(i == 0)
    def _():
        latx[0:HALO] = jnp.zeros_like(latx[0:HALO])

    for r in range(2, slab + 2):
        if r < slab:
            own_g[r].wait()
        grad_act(r)

    own_w_in.wait()
    own_b.wait()
    load_in_weights(w_in_ref, b_ref, w64)
    own_lat.wait()

    @pl.when(i < n_tm - 1)
    def _():
        lat_copy(i + 1).wait_send()

    @pl.when(i > 0)
    def _():
        lat_copy(i).wait_recv()

    def finish(r):
        frame = first + r - 2
        for tap in range(TAPS):
            row = jnp.clip(source(frame, tap) - first + HALO, 0, slab + HALO - 1)
            z[r, tap * cl : (tap + 1) * cl] = latx[row]
        z[r, TAPS * cl :] = jnp.ones((cl, width), BF16)
        pre = dot(w64[...], z[r], 1, 0)
        sig = sigmoid(pre)
        a = pre * sig
        act[r] = a.astype(BF16)
        grad_pre = (ga[r] * (sig + a * (1.0 - sig))).astype(BF16)
        gp[r] = grad_pre
        parts[r] = dot(w_in_ref[...], grad_pre, 1, 0)

    def scatter(r):
        start = clip_of(first + r - 2)
        back1 = jnp.where(start < first + r - 2, 1.0, 0.0).astype(F32)
        back2 = jnp.where(start < first + r - 3, 1.0, 0.0).astype(F32)
        p0, p1, p2 = [parts[r, tap * cl : (tap + 1) * cl] for tap in range(TAPS)]
        lg[r + 2] += p0 + (1.0 - back1) * (p1 + p2)
        lg[r + 1] += back1 * p1 + (back1 - back2) * p2
        lg[r] += back2 * p2

    lg[...] = jnp.zeros_like(lg)
    for r in range(HALO):
        finish(r)
    for r in range(HALO):
        scatter(r)
    lgh[...] = lg[0:HALO].astype(BF16)

    def halo_copy(to, p):
        return copy(lgh.at[p], tokh.at[j], s_halo.at[p], r_halo.at[j], (to, p))

    @pl.when(i > 0)
    def _():
        for p in range(n_seq):
            halo_copy(i - 1, p).start()

    @pl.when(i == n_tm - 1)
    def _():
        tokh[...] = jnp.zeros_like(tokh)

    for r in range(HALO, slab + 2):
        finish(r)
    for r in range(HALO, slab + 2):
        scatter(r)
    lgs[...] = lg[HALO : HALO + slab].astype(BF16)
    tok_copies = [copy(lgs.at[p], tok.at[j], s_tok.at[d - 1], r_tok.at[d - 1], (i, p)) for d, p in seqs]
    for c in tok_copies:
        c.start()

    rows = chans // (n_tm * n_seq)
    block = n_seq * rows

    def weight(tap):
        total = sum(
            dot(g[t], act[jnp.clip(source(first + t, tap) - first + 2, 0, slab + 1)], 1, 1) for t in range(slab)
        )
        for q in range(chips):
            for c in range(CORES):
                at = (q * CORES + c) * block
                w4[tap, c, q] = total[at : at + block].astype(BF16)

    w_core = [
        copy(w4.at[tap, other], wcore.at[tap], s_wc.at[tap], r_wc.at[tap], sibling) for tap in range(TAPS)
    ]
    w_xy = [
        [
            copy(whalf.at[tap, p], wrecv.at[tap, d - 1], s_w.at[tap, d - 1], r_w.at[tap, d - 1], (p * CORES + core, j))
            for d, p in tms
        ]
        for tap in range(TAPS)
    ]
    w_z = [
        [
            copy(wsum.at[tap, p], wrecv2.at[tap, d - 1], s_w2.at[tap, d - 1], r_w2.at[tap, d - 1], (i, p))
            for d, p in seqs
        ]
        for tap in range(TAPS)
    ]

    def weight_xy(tap):
        w_core[tap].wait()
        whalf[tap] = (w4[tap, core].astype(F32) + wcore[tap].astype(F32)).astype(BF16)
        for c in w_xy[tap]:
            c.start()

    def weight_z(tap):
        for c in w_xy[tap]:
            c.wait()
        total = whalf[tap, chip].astype(F32)
        for k in range(chips - 1):
            total = total + wrecv[tap, k].astype(F32)
        for p in range(n_seq):
            wsum[tap, p] = total[p * rows : (p + 1) * rows].astype(BF16)
        for c in w_z[tap]:
            c.start()

    def weight_end(tap):
        for c in w_z[tap]:
            c.wait()
        total = wsum[tap, j].astype(F32)
        for k in range(n_seq - 1):
            total = total + wrecv2[tap, k].astype(F32)
        wg_ref[tap] = total

    weight(0)
    w_core[0].start()
    weight(1)
    w_core[1].start()
    weight_xy(0)
    weight(2)
    w_core[2].start()
    weight_xy(1)

    own_hid.wait()
    step_rows = 128

    @pl.loop(0, hid.shape[0] // step_rows)
    def _(r):
        at = pl.ds(pl.multiple_of(r * step_rows, step_rows), step_rows)
        h = hid[at, :].astype(F32)
        center = h - jnp.mean(h, axis=1, keepdims=True)
        scaled = lax.rsqrt(jnp.mean(center * center, axis=1, keepdims=True) + 1e-06)
        nb[at, :] = (center * scaled).astype(BF16)
        inv[at, :] = jnp.broadcast_to(scaled, (step_rows, inv.shape[1]))

    misc[...] = sum(dot(z[r], gp[r], 1, 1) for r in range(slab + 2))

    n = width // PATCH
    e = cl * PATCH
    row = lax.broadcasted_iota(jnp.int32, (width, width), 0)
    col = lax.broadcasted_iota(jnp.int32, (width, width), 1)
    spread[...] = jnp.where(row == lax.rem(col, n) * PATCH + lax.div(col, n), 1.0, 0.0).astype(BF16)
    row = lax.broadcasted_iota(jnp.int32, (e, e), 0)
    col = lax.broadcasted_iota(jnp.int32, (e, e), 1)
    order = jnp.where(row == lax.rem(col, cl) * PATCH + lax.div(col, cl), 1.0, 0.0).astype(BF16)
    own_fw.wait()
    own_modu.wait()
    shift = modu_ref[0:1, :]
    scale = 1.0 + modu_ref[1:2, :]

    @pl.when(i > 0)
    def _():
        for p in range(n_seq):
            halo_copy(i - 1, p).wait_send()

    @pl.when(i < n_tm - 1)
    def _():
        for p in range(n_seq):
            copy(lgh.at[0], tokh.at[p], s_halo.at[0], r_halo.at[p], (i, j)).wait_recv()

    for c in tok_copies:
        c.wait()
    tok[j] = lgs[j]

    lat = jnp.concatenate([(tok[r].astype(F32) + tokh[r].astype(F32)).astype(BF16) for r in range(n_seq)], axis=0)
    split = dot(lat, spread[...], 1, 0)
    stack = jnp.concatenate(
        [
            jnp.concatenate([split[r * cl : (r + 1) * cl, q * n : (q + 1) * n] for r in range(n_seq)], axis=1)
            for q in range(PATCH)
        ],
        axis=0,
    )
    tg_t = dot(order, stack.astype(BF16), 1, 0)
    facc[...] = dot(tg_t.astype(BF16), nb[...], 1, 0)
    column = jnp.sum(tg_t, axis=1, keepdims=True)
    tgs[...] = tg_t.T.astype(BF16)

    fw = fw_ref[...].astype(F32)
    macc[0:1] = jnp.sum(fw * column, axis=0, keepdims=True)
    macc[1:2] = jnp.sum(fw * facc[...], axis=0, keepdims=True)
    facc[...] = facc[...] * scale + column * shift

    wf = d_model // n_tm
    wm = chans // n_tm
    er = e // n_seq
    pieces = d_model // chans
    small = jnp.concatenate(
        [misc[0 : TAPS * cl + 1, :]]
        + [macc[b : b + 1, p * chans : (p + 1) * chans] for b in range(2) for p in range(pieces)]
        + [jnp.zeros((e - TAPS * cl - 1 - 2 * pieces, chans), F32)],
        axis=0,
    )
    for a in range(n_tm):
        for b in range(n_seq):
            f4[a % CORES, a // CORES, b, :, :wf] = facc[b * er : (b + 1) * er, a * wf : (a + 1) * wf].astype(BF16)
            f4[a % CORES, a // CORES, b, :, wf : wf + wm] = small[b * er : (b + 1) * er, a * wm : (a + 1) * wm].astype(BF16)
            if wf + wm < f4.shape[4]:
                f4[a % CORES, a // CORES, b, :, wf + wm :] = jnp.zeros((er, f4.shape[4] - wf - wm), BF16)
    f_core = copy(f4.at[other], fcore, s_fc, r_fc, sibling)
    f_core.start()

    half = hid.shape[0] // 2

    def input_gradient(k):
        at = slice(k * half, (k + 1) * half)
        normed = nb[at, :].astype(F32)
        ng = dot(tgs[at, :], fw_ref[...], 1, 0) * scale
        m1 = jnp.mean(ng, axis=1, keepdims=True)
        m2 = jnp.mean(ng * normed, axis=1, keepdims=True)
        dx_ref[at, :] = (inv[at, 0:1] * (ng - m1 - normed * m2)).astype(BF16)

    input_gradient(0)
    f_core.wait()
    for q in range(chips):
        fhalf[q] = (f4[core, q].astype(F32) + fcore[q].astype(F32)).astype(BF16)
    f_copies = [
        copy(fhalf.at[p], frecv.at[d - 1], s_f.at[d - 1], r_f.at[d - 1], (p * CORES + core, j))
        for d, p in tms
    ]
    for c in f_copies:
        c.start()
    weight_xy(2)
    input_gradient(1)
    weight_z(0)
    weight_z(1)
    for c in f_copies:
        c.wait()
    total = fhalf[chip].astype(F32)
    for k in range(chips - 1):
        total = total + frecv[k].astype(F32)
    fsum[...] = total.astype(BF16)
    f2_copies = [
        copy(fsum.at[p], frecv2.at[d - 1], s_f2.at[d - 1], r_f2.at[d - 1], (i, p)) for d, p in seqs
    ]
    for c in f2_copies:
        c.start()
    weight_z(2)
    for c in f2_copies:
        c.wait()
    total = fsum[j].astype(F32)
    for k in range(n_seq - 1):
        total = total + frecv2[k].astype(F32)
    gath[core, chip, j] = total.astype(BF16)
    g_copies = [
        copy(gath.at[core, chip, j], gath.at[core, chip, j], s_g.at[d - 1], r_g.at[d - 1], (i, p)) for d, p in seqs
    ]
    for c in g_copies:
        c.start()
    weight_end(0)
    weight_end(1)
    for c in g_copies:
        c.wait()
    g2_copies = [
        copy(gath.at[core, chip], gath.at[core, chip], s_g2.at[d - 1], r_g2.at[d - 1], (p * CORES + core, j))
        for d, p in tms
    ]
    for c in g2_copies:
        c.start()
    weight_end(2)
    for c in g2_copies:
        c.wait()
    g_core = copy(gath.at[core], gath.at[core], s_gc, r_gc, sibling)
    g_core.start()
    g_core.wait()


def unpack_kernel(gath, wg_ref, dx_in, fin_ref, mod_ref, in_ref, bias_ref, wg_out, dx_hbm, small, sem):
    dx_copy = pltpu.make_async_copy(dx_in, dx_hbm, sem)
    dx_copy.start()
    cores, chips, n_seq, er, _ = gath.shape
    n_tm = cores * chips
    d_model = fin_ref.shape[1]
    taps_cl, chans = in_ref.shape
    wf = d_model // n_tm
    wm = chans // n_tm
    pieces = d_model // chans
    for a in range(n_tm):
        for b in range(n_seq):
            fin_ref[b * er : (b + 1) * er, a * wf : (a + 1) * wf] = gath[a % cores, a // cores, b, :, :wf].astype(F32)
            small[b * er : (b + 1) * er, a * wm : (a + 1) * wm] = gath[a % cores, a // cores, b, :, wf : wf + wm].astype(F32)
    in_ref[...] = small[:taps_cl, :]
    bias_ref[...] = small[taps_cl : taps_cl + 1, :]
    for b in range(2):
        for p in range(pieces):
            at = taps_cl + 1 + b * pieces + p
            mod_ref[b : b + 1, p * chans : (p + 1) * chans] = small[at : at + 1, :]
    wg_out[...] = wg_ref[...]
    dx_copy.wait()


def local(n_tm, n_seq, latents, hidden, grad_out, conv_in_w, conv_in_b, conv_w, final_w, modulation, clip_start):
    slab, cl, width = latents.shape
    taps, chans = conv_w.shape[:2]
    tokens, d_model = hidden.shape
    rows = chans // (n_tm * n_seq)
    block = n_seq * rows
    chips = n_tm // CORES
    w_in = conv_in_w.transpose(0, 2, 1).reshape(taps * cl, chans)
    bias = conv_in_b.reshape(1, chans)
    e = cl * PATCH
    er = e // n_seq
    cw = -(-((d_model + chans) // n_tm) // 128) * 128
    vmem = pl.BlockSpec(memory_space=pltpu.VMEM)
    hbm = pl.BlockSpec(memory_space=pltpu.HBM)
    smem = pl.BlockSpec(memory_space=pltpu.SMEM)
    dma = pltpu.SemaphoreType.DMA
    nt, ns = chips - 1, n_seq - 1

    def b16(*shape):
        return pltpu.VMEM(shape, BF16)

    def f32(*shape):
        return pltpu.VMEM(shape, F32)

    def in_hbm(x):
        return pltpu.with_memory_space_constraint(x, pltpu.HBM)

    dx, wg, gath = pl.pallas_call(
        functools.partial(main_kernel, n_tm, n_seq),
        out_shape=(
            b16(tokens, d_model),
            f32(taps, rows, chans),
            b16(CORES, chips, n_seq, er, cw),
        ),
        in_specs=[hbm] * 9,
        out_specs=(vmem, vmem, vmem),
        scratch_shapes=[
            pltpu.SMEM(clip_start.shape, jnp.int32),
            b16(taps * cl, chans),
            f32(1, chans),
            b16(e, d_model),
            f32(2, d_model),
            b16(slab + HALO, cl, width),
            b16(slab, chans, width),
            b16(tokens, d_model),
            b16(tokens, d_model),
            f32(tokens, 128),
            b16(chans, 4 * cl),
            b16(slab + 2, 4 * cl, width),
            b16(taps + 3, chans, chans),
            b16(slab + 2, chans, width),
            f32(slab + 2, chans, width),
            b16(slab + 2, chans, width),
            f32(slab + 2, taps * cl, width),
            f32(4 * cl, chans),
            f32(slab + HALO, cl, width),
            b16(HALO, cl, width),
            b16(slab, cl, width),
            b16(n_seq, cl, width),
            b16(n_seq, cl, width),
            b16(taps, CORES, chips, block, chans),
            b16(taps, chips, block, chans),
            b16(taps, chips, block, chans),
            b16(taps, nt, block, chans),
            b16(taps, n_seq, rows, chans),
            b16(taps, ns, rows, chans),
            b16(width, width),
            b16(tokens, e),
            f32(e, d_model),
            f32(8, d_model),
            b16(CORES, chips, n_seq, er, cw),
            b16(chips, n_seq, er, cw),
            b16(chips, n_seq, er, cw),
            b16(nt, n_seq, er, cw),
            b16(n_seq, er, cw),
            b16(ns, er, cw),
            dma((8,)), dma((slab,)), dma(()), dma(()), dma((n_seq,)), dma((n_seq,)), dma((ns,)), dma((ns,)),
            dma((taps,)), dma((taps,)), dma((taps, nt)), dma((taps, nt)), dma((taps, ns)), dma((taps, ns)),
            dma(()), dma(()), dma((nt,)), dma((nt,)), dma((ns,)), dma((ns,)),
            dma((ns,)), dma((ns,)), dma((nt,)), dma((nt,)), dma(()), dma(()),
        ],
        compiler_params=pltpu.CompilerParams(
            vmem_limit_bytes=MAIN_VMEM, collective_id=0, has_side_effects=True
        ),
        name="main",
    )(*[in_hbm(x) for x in (clip_start, latents, hidden, grad_out, w_in, bias, conv_w, final_w.T, modulation)])
    fin, mod, w_in_grad, bias_grad, wg, dx = pl.pallas_call(
        unpack_kernel,
        out_shape=(
            jax.ShapeDtypeStruct((e, d_model), F32),
            jax.ShapeDtypeStruct((2, d_model), F32),
            jax.ShapeDtypeStruct((taps * cl, chans), F32),
            jax.ShapeDtypeStruct((1, chans), F32),
            jax.ShapeDtypeStruct((taps, rows, chans), F32),
            jax.ShapeDtypeStruct((tokens, d_model), BF16),
        ),
        in_specs=[vmem, vmem, vmem],
        out_specs=(vmem,) * 5 + (hbm,),
        scratch_shapes=[pltpu.VMEM((e, chans), F32), dma(())],
        compiler_params=pltpu.CompilerParams(vmem_limit_bytes=SMALL_VMEM),
        name="unpack",
    )(gath, wg, dx)
    return (
        dx,
        wg.transpose(1, 0, 2),
        w_in_grad.reshape(taps, cl, chans).transpose(0, 2, 1),
        bias_grad.reshape(chans),
        fin.T,
        mod,
    )


def solution(mesh):
    return jax.shard_map(
        functools.partial(local, mesh.shape["tm"], mesh.shape["seq"]),
        mesh=mesh,
        in_specs=(
            P("tm", None, "seq"),
            P(("tm", "seq"), None),
            P("tm", None, "seq"),
            P(),
            P(),
            P(),
            P(),
            P(),
            P(),
        ),
        out_specs=(P(("tm", "seq"), None), P(("tm", "seq"), None, None), P(), P(), P(), P()),
        check_vma=False,
    )
```

```python
import functools

import jax
import jax.numpy as jnp
from jax import lax
from jax.experimental import pallas as pl
from jax.experimental.pallas import tpu as pltpu
from jax.sharding import PartitionSpec as P

F32 = jnp.float32
BF16 = jnp.bfloat16
MESH = pl.DeviceIdType.MESH
PATCH = 4
CORES = 2
TAPS = 3
HALO = 4
CHUNKS = 2
MAIN_VMEM = 46 * 1024 * 1024
SMALL_VMEM = 12 * 1024 * 1024


def dot(a, b, ca, cb):
    return lax.dot_general(a, b, (((ca,), (cb,)), ((), ())), preferred_element_type=F32)


def load_in_weights(w_in_ref, b_ref, w64):
    bias = b_ref[...]
    hi = bias.astype(BF16)
    mid = (bias - hi.astype(F32)).astype(BF16)
    lo = (bias - hi.astype(F32) - mid.astype(F32)).astype(BF16)
    pad = jnp.zeros((16 - 3, bias.shape[1]), F32)
    rows = jnp.concatenate(
        [w_in_ref[...].astype(F32), hi.astype(F32), mid.astype(F32), lo.astype(F32), pad], axis=0
    )
    w64[...] = rows.T.astype(BF16)


def pieces_of(wf, wm, cw, width):
    for lo, hi, kind in ((0, wf, 0), (wf, wf + wm, 1), (wf + wm, cw, 2)):
        while lo < hi:
            end = min(hi, (lo // width + 1) * width)
            yield kind, lo, end, lo // width, lo % width
            lo = end


def sigmoid(x):
    return 0.5 * jnp.tanh(0.5 * x) + 0.5


def main_kernel(
    n_tm, n_seq,
    clip_hbm, lat_hbm, hid_hbm, grad_hbm, w_in_hbm, b_hbm, w_hbm, fw_hbm, modu_hbm,
    dx_ref, wg_ref, gath,
    clip_ref, w_in_ref, b_ref, fw_ref, modu_ref,
    latx, lat_own, slope, g, hid, nb, inv, w64, z, tab, act, ga, gp, parts, misc, lg, lgh, lgs, tok, tokh,
    w4, wcore, whalf, wrecv, wsum, wrecv2,
    spread, tgs, facc, macc, f4, fcore, fhalf, frecv, fsum, frecv2,
    s_in, s_g_in, s_lat, r_lat, s_halo, r_halo, s_tok, r_tok,
    s_wc, r_wc, s_w, r_w, s_w2, r_w2,
    s_fc, r_fc, s_f, r_f, s_f2, r_f2, s_g, r_g, s_g2, r_g2, s_gc, r_gc,
):
    i = lax.axis_index("tm")
    j = lax.axis_index("seq")
    chips = n_tm // CORES
    core = lax.rem(i, CORES)
    chip = lax.div(i, CORES)
    other = CORES - 1 - core
    sibling = (chip * CORES + other, j)
    tms = [(d, lax.rem(chip + d, chips)) for d in range(1, chips)]
    seqs = [(d, lax.rem(j + d, n_seq)) for d in range(1, n_seq)]
    slab, chans = g.shape[:2]
    cl, width = latx.shape[1:]
    frames = clip_ref.shape[0]
    d_model = hid.shape[1]
    first = i * slab

    loads = [
        pltpu.make_async_copy(src, dst, s_in.at[k])
        for k, (src, dst) in enumerate(
            [
                (clip_hbm, clip_ref),
                (w_hbm, tab.at[pl.ds(0, TAPS)]),
                (w_in_hbm, w_in_ref),
                (b_hbm, b_ref),
                (lat_hbm, latx.at[pl.ds(HALO, slab)]),
                (hid_hbm, hid),
                (fw_hbm, fw_ref),
                (modu_hbm, modu_ref),
                (lat_hbm, lat_own),
            ]
        )
    ]
    own_clip, own_w, own_w_in, own_b, own_lat, own_hid, own_fw, own_modu, own_lat2 = loads
    own_g = [pltpu.make_async_copy(grad_hbm.at[t], g.at[t], s_g_in.at[t]) for t in range(slab)]
    for c in [own_w_in, own_b, own_lat2, own_clip, own_w] + own_g + [own_lat, own_fw, own_modu, own_hid]:
        c.start()

    barrier = pltpu.get_barrier_semaphore()
    greeted = [(p * CORES + core, j) for _, p in tms] + [sibling] + [(i, p) for _, p in seqs]
    greeted += [(lax.rem(i + 1, n_tm), p) for p in range(n_seq)] + [(lax.rem(i + n_tm - 1, n_tm), j)]
    for to in greeted:
        pl.semaphore_signal(barrier, inc=1, device_id=to, device_id_type=MESH)

    def copy(src, dst, send, recv, to):
        return pltpu.make_async_remote_copy(
            src_ref=src, dst_ref=dst, send_sem=send, recv_sem=recv, device_id=to, device_id_type=MESH
        )

    def lat_copy(to):
        return copy(lat_hbm.at[pl.ds(slab - HALO, HALO)], latx.at[pl.ds(0, HALO)], s_lat, r_lat, (to, j))

    def clip_of(frame):
        return clip_ref[jnp.clip(frame, 0, frames - 1)]

    def source(frame, tap):
        return jnp.maximum(frame - tap, clip_of(frame))

    n = width // PATCH
    e = cl * PATCH
    row = lax.broadcasted_iota(jnp.int32, (width, width), 0)
    col = lax.broadcasted_iota(jnp.int32, (width, width), 1)
    spread[...] = jnp.where(row == lax.rem(col, n) * PATCH + lax.div(col, n), 1.0, 0.0).astype(BF16)
    row = lax.broadcasted_iota(jnp.int32, (e, e), 0)
    col = lax.broadcasted_iota(jnp.int32, (e, e), 1)
    order = jnp.where(row == lax.rem(col, cl) * PATCH + lax.div(col, cl), 1.0, 0.0).astype(BF16)
    def prepare(r, held, base):
        frame = first + r - 2
        for tap in range(TAPS):
            row = jnp.clip(source(frame, tap) - base, 0, held.shape[0] - 1)
            z[r, tap * cl : (tap + 1) * cl] = held[row]
        z[r, TAPS * cl :] = jnp.ones((cl, width), BF16)
        pre = dot(w64[...], z[r], 1, 0)
        sig = sigmoid(pre)
        a = pre * sig
        act[r] = a.astype(BF16)
        return sig + a * (1.0 - sig)

    own_w_in.wait()
    own_b.wait()
    load_in_weights(w_in_ref, b_ref, w64)
    own_clip.wait()
    own_lat2.wait()
    for r in range(HALO, slab + 2):
        slope[r - HALO] = prepare(r, lat_own, first)
    own_w.wait()
    later = tab[1].astype(F32) + tab[2].astype(F32)
    tab[TAPS] = later.astype(BF16)
    tab[TAPS + 1] = (later + tab[0].astype(F32)).astype(BF16)
    tab[TAPS + 2] = jnp.zeros_like(tab[TAPS + 2])

    def choice(t, back):
        start = clip_of(first + t)
        back1 = start < first + t
        back2 = start < first + t - 1
        if back == 0:
            return jnp.where(back1, 0, TAPS + 1)
        if back == 1:
            return jnp.where(back2, 1, jnp.where(back1, TAPS, TAPS + 2))
        return jnp.where(back2, 2, TAPS + 2)

    def grad_act(r):
        ga[r] = sum(
            dot(tab[choice(r - 2 + back, back)], g[r - 2 + back], 0, 0)
            for back in range(TAPS)
            if 0 <= r - 2 + back < slab
        )

    own_g[0].wait()
    grad_act(0)
    own_g[1].wait()
    grad_act(1)
    pl.semaphore_wait(barrier, len(greeted))

    @pl.when(i < n_tm - 1)
    def _():
        lat_copy(i + 1).start()

    @pl.when(i == 0)
    def _():
        latx[0:HALO] = jnp.zeros_like(latx[0:HALO])

    for r in range(2, slab + 2):
        if r < slab:
            own_g[r].wait()
        grad_act(r)

    own_lat.wait()

    @pl.when(i < n_tm - 1)
    def _():
        lat_copy(i + 1).wait_send()

    @pl.when(i > 0)
    def _():
        lat_copy(i).wait_recv()

    def finish(r):
        factor = prepare(r, latx, first - HALO) if r < HALO else slope[r - HALO]
        grad_pre = (ga[r] * factor).astype(BF16)
        gp[r] = grad_pre
        parts[r] = dot(w_in_ref[...], grad_pre, 1, 0)

    def scatter(r):
        start = clip_of(first + r - 2)
        back1 = jnp.where(start < first + r - 2, 1.0, 0.0).astype(F32)
        back2 = jnp.where(start < first + r - 3, 1.0, 0.0).astype(F32)
        p0, p1, p2 = [parts[r, tap * cl : (tap + 1) * cl] for tap in range(TAPS)]
        lg[r + 2] += p0 + (1.0 - back1) * (p1 + p2)
        lg[r + 1] += back1 * p1 + (back1 - back2) * p2
        lg[r] += back2 * p2

    lg[...] = jnp.zeros_like(lg)
    for r in range(HALO):
        finish(r)
    for r in range(HALO):
        scatter(r)
    lgh[...] = lg[0:HALO].astype(BF16)

    def halo_copy(to, p):
        return copy(lgh.at[p], tokh.at[j], s_halo.at[p], r_halo.at[j], (to, p))

    @pl.when(i > 0)
    def _():
        for p in range(n_seq):
            halo_copy(i - 1, p).start()

    @pl.when(i == n_tm - 1)
    def _():
        tokh[...] = jnp.zeros_like(tokh)

    for r in range(HALO, slab + 2):
        finish(r)
    for r in range(HALO, slab + 2):
        scatter(r)
    lgs[...] = lg[HALO : HALO + slab].astype(BF16)
    tok_copies = [copy(lgs.at[p], tok.at[j], s_tok.at[d - 1], r_tok.at[d - 1], (i, p)) for d, p in seqs]
    for c in tok_copies:
        c.start()

    rows = chans // (n_tm * n_seq)
    block = n_seq * rows

    def weight(tap):
        total = sum(
            dot(g[t], act[jnp.clip(source(first + t, tap) - first + 2, 0, slab + 1)], 1, 1) for t in range(slab)
        )
        for q in range(chips):
            for c in range(CORES):
                at = (q * CORES + c) * block
                w4[tap, c, q] = total[at : at + block].astype(BF16)

    w_core = [
        copy(w4.at[tap, other], wcore.at[tap], s_wc.at[tap], r_wc.at[tap], sibling) for tap in range(TAPS)
    ]
    w_xy = [
        [
            copy(whalf.at[tap, p], wrecv.at[tap, d - 1], s_w.at[tap, d - 1], r_w.at[tap, d - 1], (p * CORES + core, j))
            for d, p in tms
        ]
        for tap in range(TAPS)
    ]
    w_z = [
        [
            copy(wsum.at[tap, p], wrecv2.at[tap, d - 1], s_w2.at[tap, d - 1], r_w2.at[tap, d - 1], (i, p))
            for d, p in seqs
        ]
        for tap in range(TAPS)
    ]

    def weight_xy(tap):
        w_core[tap].wait()
        whalf[tap] = (w4[tap, core].astype(F32) + wcore[tap].astype(F32)).astype(BF16)
        for c in w_xy[tap]:
            c.start()

    def weight_z(tap):
        for c in w_xy[tap]:
            c.wait()
        total = whalf[tap, chip].astype(F32)
        for k in range(chips - 1):
            total = total + wrecv[tap, k].astype(F32)
        for p in range(n_seq):
            wsum[tap, p] = total[p * rows : (p + 1) * rows].astype(BF16)
        for c in w_z[tap]:
            c.start()

    def weight_end(tap):
        for c in w_z[tap]:
            c.wait()
        total = wsum[tap, j].astype(F32)
        for k in range(n_seq - 1):
            total = total + wrecv2[tap, k].astype(F32)
        wg_ref[tap] = total

    weight(0)
    w_core[0].start()
    own_hid.wait()
    step_rows = 128

    @pl.loop(0, hid.shape[0] // step_rows)
    def _(r):
        at = pl.ds(pl.multiple_of(r * step_rows, step_rows), step_rows)
        h = hid[at, :].astype(F32)
        center = h - jnp.mean(h, axis=1, keepdims=True)
        scaled = lax.rsqrt(jnp.mean(center * center, axis=1, keepdims=True) + 1e-06)
        nb[at, :] = (center * scaled).astype(BF16)
        inv[at, :] = jnp.broadcast_to(scaled, (step_rows, inv.shape[1]))

    weight_xy(0)
    weight(1)
    w_core[1].start()
    misc[...] = sum(dot(z[r], gp[r], 1, 1) for r in range(slab + 2))
    weight_xy(1)

    own_fw.wait()
    own_modu.wait()
    shift = modu_ref[0:1, :]
    scale = 1.0 + modu_ref[1:2, :]

    @pl.when(i > 0)
    def _():
        for p in range(n_seq):
            halo_copy(i - 1, p).wait_send()

    @pl.when(i < n_tm - 1)
    def _():
        for p in range(n_seq):
            copy(lgh.at[0], tokh.at[p], s_halo.at[0], r_halo.at[p], (i, j)).wait_recv()

    for c in tok_copies:
        c.wait()
    tok[j] = lgs[j]

    lat = jnp.concatenate([(tok[r].astype(F32) + tokh[r].astype(F32)).astype(BF16) for r in range(n_seq)], axis=0)
    split = dot(lat, spread[...], 1, 0)
    stack = jnp.concatenate(
        [
            jnp.concatenate([split[r * cl : (r + 1) * cl, q * n : (q + 1) * n] for r in range(n_seq)], axis=1)
            for q in range(PATCH)
        ],
        axis=0,
    )
    tg_t = dot(order, stack.astype(BF16), 1, 0)
    facc[...] = dot(tg_t.astype(BF16), nb[...], 1, 0)
    column = jnp.sum(tg_t, axis=1, keepdims=True)
    tgs[...] = tg_t.T.astype(BF16)

    fw = fw_ref[...].astype(F32)
    macc[0:1] = jnp.sum(fw * column, axis=0, keepdims=True)
    macc[1:2] = jnp.sum(fw * facc[...], axis=0, keepdims=True)
    facc[...] = facc[...] * scale + column * shift

    wf = d_model // n_tm
    wm = chans // n_tm
    er = e // n_seq
    pieces = d_model // chans
    small = jnp.concatenate(
        [misc[0 : TAPS * cl + 1, :]]
        + [macc[b : b + 1, p * chans : (p + 1) * chans] for b in range(2) for p in range(pieces)]
        + [jnp.zeros((e - TAPS * cl - 1 - 2 * pieces, chans), F32)],
        axis=0,
    )
    nc, cwc = f4.shape[0], f4.shape[5]
    for a in range(n_tm):
        for b in range(n_seq):
            at = slice(b * er, (b + 1) * er)
            for kind, lo, hi, c, off in pieces_of(wf, wm, nc * cwc, cwc):
                if kind == 0:
                    value = facc[at, a * wf + lo : a * wf + hi]
                elif kind == 1:
                    value = small[at, a * wm + lo - wf : a * wm + hi - wf]
                else:
                    value = jnp.zeros((er, hi - lo), F32)
                f4[c, a % CORES, a // CORES, b, :, off : off + hi - lo] = value.astype(BF16)
    chunks = range(nc)
    f_core = [copy(f4.at[c, other], fcore.at[c], s_fc.at[c], r_fc.at[c], sibling) for c in chunks]
    for c in chunks:
        f_core[c].start()

    half = hid.shape[0] // 2

    def input_gradient(k):
        at = slice(k * half, (k + 1) * half)
        normed = nb[at, :].astype(F32)
        ng = dot(tgs[at, :], fw_ref[...], 1, 0) * scale
        m1 = jnp.mean(ng, axis=1, keepdims=True)
        m2 = jnp.mean(ng * normed, axis=1, keepdims=True)
        dx_ref[at, :] = (inv[at, 0:1] * (ng - m1 - normed * m2)).astype(BF16)

    f_xy = [
        [
            copy(fhalf.at[c, p], frecv.at[c, d - 1], s_f.at[c, d - 1], r_f.at[c, d - 1], (p * CORES + core, j))
            for d, p in tms
        ]
        for c in chunks
    ]
    f_z = [
        [copy(fsum.at[c, p], frecv2.at[c, d - 1], s_f2.at[c, d - 1], r_f2.at[c, d - 1], (i, p)) for d, p in seqs]
        for c in chunks
    ]
    g_z = [
        [
            copy(
                gath.at[c, core, chip, j], gath.at[c, core, chip, j], s_g.at[c, d - 1], r_g.at[c, d - 1], (i, p)
            )
            for d, p in seqs
        ]
        for c in chunks
    ]
    g_xy = [
        [
            copy(
                gath.at[c, core, chip], gath.at[c, core, chip], s_g2.at[c, d - 1], r_g2.at[c, d - 1],
                (p * CORES + core, j),
            )
            for d, p in tms
        ]
        for c in chunks
    ]
    g_core = [copy(gath.at[c, core], gath.at[c, core], s_gc.at[c], r_gc.at[c], sibling) for c in chunks]

    def start(copies):
        for c in copies:
            c.start()

    def wait(copies):
        for c in copies:
            c.wait()

    def final_xy(c):
        f_core[c].wait()
        for q in range(chips):
            fhalf[c, q] = (f4[c, core, q].astype(F32) + fcore[c, q].astype(F32)).astype(BF16)
        start(f_xy[c])

    def final_z(c):
        wait(f_xy[c])
        total = fhalf[c, chip].astype(F32)
        for k in range(chips - 1):
            total = total + frecv[c, k].astype(F32)
        fsum[c] = total.astype(BF16)
        start(f_z[c])

    def gather_z(c):
        wait(f_z[c])
        total = fsum[c, j].astype(F32)
        for k in range(n_seq - 1):
            total = total + frecv2[c, k].astype(F32)
        gath[c, core, chip, j] = total.astype(BF16)
        start(g_z[c])

    def gather_xy(c):
        wait(g_z[c])
        start(g_xy[c])

    def gather_core(c):
        wait(g_xy[c])
        g_core[c].start()

    weight(2)
    w_core[2].start()
    for c in chunks:
        final_xy(c)
    weight_z(0)
    input_gradient(0)
    weight_z(1)
    input_gradient(1)
    for c in chunks:
        final_z(c)
    weight_xy(2)
    for c in chunks:
        gather_z(c)
    weight_end(0)
    weight_end(1)
    for c in chunks:
        gather_xy(c)
    weight_z(2)
    for c in chunks:
        gather_core(c)
    weight_end(2)
    wait(g_core)


def unpack_kernel(gath, wg_ref, dx_in, fin_ref, mod_ref, in_ref, bias_ref, wg_out, dx_hbm, small, sem):
    dx_copy = pltpu.make_async_copy(dx_in, dx_hbm, sem)
    dx_copy.start()
    nc, cores, chips, n_seq, er, cwc = gath.shape
    n_tm = cores * chips
    d_model = fin_ref.shape[1]
    taps_cl, chans = in_ref.shape
    wf = d_model // n_tm
    wm = chans // n_tm
    pieces = d_model // chans
    for a in range(n_tm):
        for b in range(n_seq):
            at = slice(b * er, (b + 1) * er)
            for kind, lo, hi, c, off in pieces_of(wf, wm, wf + wm, cwc):
                value = gath[c, a % cores, a // cores, b, :, off : off + hi - lo].astype(F32)
                if kind == 0:
                    fin_ref[at, a * wf + lo : a * wf + hi] = value
                else:
                    small[at, a * wm + lo - wf : a * wm + hi - wf] = value
    in_ref[...] = small[:taps_cl, :]
    bias_ref[...] = small[taps_cl : taps_cl + 1, :]
    for b in range(2):
        for p in range(pieces):
            at = taps_cl + 1 + b * pieces + p
            mod_ref[b : b + 1, p * chans : (p + 1) * chans] = small[at : at + 1, :]
    wg_out[...] = wg_ref[...]
    dx_copy.wait()


def local(n_tm, n_seq, latents, hidden, grad_out, conv_in_w, conv_in_b, conv_w, final_w, modulation, clip_start):
    slab, cl, width = latents.shape
    taps, chans = conv_w.shape[:2]
    tokens, d_model = hidden.shape
    rows = chans // (n_tm * n_seq)
    block = n_seq * rows
    chips = n_tm // CORES
    w_in = conv_in_w.transpose(0, 2, 1).reshape(taps * cl, chans)
    bias = conv_in_b.reshape(1, chans)
    e = cl * PATCH
    er = e // n_seq
    lanes = -(-((d_model + chans) // n_tm) // 128)
    nc = max(c for c in range(1, CHUNKS + 1) if lanes % c == 0)
    cw = lanes // nc * 128
    vmem = pl.BlockSpec(memory_space=pltpu.VMEM)
    hbm = pl.BlockSpec(memory_space=pltpu.HBM)
    smem = pl.BlockSpec(memory_space=pltpu.SMEM)
    dma = pltpu.SemaphoreType.DMA
    nt, ns = chips - 1, n_seq - 1

    def b16(*shape):
        return pltpu.VMEM(shape, BF16)

    def f32(*shape):
        return pltpu.VMEM(shape, F32)

    def in_hbm(x):
        return pltpu.with_memory_space_constraint(x, pltpu.HBM)

    dx, wg, gath = pl.pallas_call(
        functools.partial(main_kernel, n_tm, n_seq),
        out_shape=(
            b16(tokens, d_model),
            f32(taps, rows, chans),
            b16(nc, CORES, chips, n_seq, er, cw),
        ),
        in_specs=[hbm] * 9,
        out_specs=(vmem, vmem, vmem),
        scratch_shapes=[
            pltpu.SMEM(clip_start.shape, jnp.int32),
            b16(taps * cl, chans),
            f32(1, chans),
            b16(e, d_model),
            f32(2, d_model),
            b16(slab + HALO, cl, width),
            b16(slab, cl, width),
            f32(slab + 2 - HALO, chans, width),
            b16(slab, chans, width),
            b16(tokens, d_model),
            b16(tokens, d_model),
            f32(tokens, 128),
            b16(chans, 4 * cl),
            b16(slab + 2, 4 * cl, width),
            b16(taps + 3, chans, chans),
            b16(slab + 2, chans, width),
            f32(slab + 2, chans, width),
            b16(slab + 2, chans, width),
            f32(slab + 2, taps * cl, width),
            f32(4 * cl, chans),
            f32(slab + HALO, cl, width),
            b16(HALO, cl, width),
            b16(slab, cl, width),
            b16(n_seq, cl, width),
            b16(n_seq, cl, width),
            b16(taps, CORES, chips, block, chans),
            b16(taps, chips, block, chans),
            b16(taps, chips, block, chans),
            b16(taps, nt, block, chans),
            b16(taps, n_seq, rows, chans),
            b16(taps, ns, rows, chans),
            b16(width, width),
            b16(tokens, e),
            f32(e, d_model),
            f32(8, d_model),
            b16(nc, CORES, chips, n_seq, er, cw),
            b16(nc, chips, n_seq, er, cw),
            b16(nc, chips, n_seq, er, cw),
            b16(nc, nt, n_seq, er, cw),
            b16(nc, n_seq, er, cw),
            b16(nc, ns, er, cw),
            dma((9,)), dma((slab,)), dma(()), dma(()), dma((n_seq,)), dma((n_seq,)), dma((ns,)), dma((ns,)),
            dma((taps,)), dma((taps,)), dma((taps, nt)), dma((taps, nt)), dma((taps, ns)), dma((taps, ns)),
            dma((nc,)), dma((nc,)), dma((nc, nt)), dma((nc, nt)), dma((nc, ns)), dma((nc, ns)),
            dma((nc, ns)), dma((nc, ns)), dma((nc, nt)), dma((nc, nt)), dma((nc,)), dma((nc,)),
        ],
        compiler_params=pltpu.CompilerParams(
            vmem_limit_bytes=MAIN_VMEM, collective_id=0, has_side_effects=True
        ),
        name="main",
    )(*[in_hbm(x) for x in (clip_start, latents, hidden, grad_out, w_in, bias, conv_w, final_w.T, modulation)])
    fin, mod, w_in_grad, bias_grad, wg, dx = pl.pallas_call(
        unpack_kernel,
        out_shape=(
            jax.ShapeDtypeStruct((e, d_model), F32),
            jax.ShapeDtypeStruct((2, d_model), F32),
            jax.ShapeDtypeStruct((taps * cl, chans), F32),
            jax.ShapeDtypeStruct((1, chans), F32),
            jax.ShapeDtypeStruct((taps, rows, chans), F32),
            jax.ShapeDtypeStruct((tokens, d_model), BF16),
        ),
        in_specs=[vmem, vmem, vmem],
        out_specs=(vmem,) * 5 + (hbm,),
        scratch_shapes=[pltpu.VMEM((e, chans), F32), dma(())],
        compiler_params=pltpu.CompilerParams(vmem_limit_bytes=SMALL_VMEM),
        name="unpack",
    )(gath, wg, dx)
    return (
        dx,
        wg.transpose(1, 0, 2),
        w_in_grad.reshape(taps, cl, chans).transpose(0, 2, 1),
        bias_grad.reshape(chans),
        fin.T,
        mod,
    )


def solution(mesh):
    return jax.shard_map(
        functools.partial(local, mesh.shape["tm"], mesh.shape["seq"]),
        mesh=mesh,
        in_specs=(
            P("tm", None, "seq"),
            P(("tm", "seq"), None),
            P("tm", None, "seq"),
            P(),
            P(),
            P(),
            P(),
            P(),
            P(),
        ),
        out_specs=(P(("tm", "seq"), None), P(("tm", "seq"), None, None), P(), P(), P(), P()),
        check_vma=False,
    )
```

```python
import functools

import jax
import jax.numpy as jnp
from jax import lax
from jax.experimental import pallas as pl
from jax.experimental.pallas import tpu as pltpu
from jax.sharding import PartitionSpec as P

F32 = jnp.float32
BF16 = jnp.bfloat16
MESH = pl.DeviceIdType.MESH
PATCH = 4
CORES = 2
TAPS = 3
HALO = 4
CHUNKS = 2
MAIN_VMEM = 46 * 1024 * 1024
SMALL_VMEM = 12 * 1024 * 1024


def dot(a, b, ca, cb):
    return lax.dot_general(a, b, (((ca,), (cb,)), ((), ())), preferred_element_type=F32)


def load_in_weights(w_in_ref, b_ref, w64):
    bias = b_ref[...]
    hi = bias.astype(BF16)
    mid = (bias - hi.astype(F32)).astype(BF16)
    lo = (bias - hi.astype(F32) - mid.astype(F32)).astype(BF16)
    pad = jnp.zeros((16 - 3, bias.shape[1]), F32)
    rows = jnp.concatenate(
        [w_in_ref[...].astype(F32), hi.astype(F32), mid.astype(F32), lo.astype(F32), pad], axis=0
    )
    w64[...] = rows.T.astype(BF16)


def places(n_tm, groups, nc, width, wide, narrow):
    parts = n_tm // groups
    for a in range(n_tm):
        for c in range(nc):
            lo = ((a % parts) * nc + c) * width
            mid = min(max(lo, wide), lo + width)
            end = min(max(lo, wide + narrow), lo + width)
            yield a, c, a // parts, lo, mid, end


def sigmoid(x):
    return 0.5 * jnp.tanh(0.5 * x) + 0.5


def main_kernel(
    n_tm, n_seq,
    clip_hbm, lat_hbm, hid_hbm, grad_hbm, w_in_hbm, b_hbm, w_hbm, fw_hbm, modu_hbm,
    dx_ref, wg_ref, gath,
    clip_ref, w_in_ref, b_ref, fw_ref, modu_ref,
    latx, lat_own, slope, g, hid, nb, inv, w64, z, tab, act, ga, gp, parts, misc, lg, lgh, lgs, tok, tokh,
    w4, wcore, whalf, wrecv, wsum, wrecv2,
    spread, tgs, facc, macc, f4, fcore, fhalf, frecv, fall,
    s_in, s_g_in, s_lat, r_lat, s_halo, r_halo, s_tok, r_tok,
    s_wc, r_wc, s_w, r_w, s_w2, r_w2,
    s_fc, r_fc, s_f, r_f, s_f2, r_f2, s_g, r_g, s_gc, r_gc,
):
    i = lax.axis_index("tm")
    j = lax.axis_index("seq")
    chips = n_tm // CORES
    core = lax.rem(i, CORES)
    chip = lax.div(i, CORES)
    other = CORES - 1 - core
    sibling = (chip * CORES + other, j)
    tms = [(d, lax.rem(chip + d, chips)) for d in range(1, chips)]
    seqs = [(d, lax.rem(j + d, n_seq)) for d in range(1, n_seq)]
    slab, chans = g.shape[:2]
    cl, width = latx.shape[1:]
    frames = clip_ref.shape[0]
    d_model = hid.shape[1]
    first = i * slab

    loads = [
        pltpu.make_async_copy(src, dst, s_in.at[k])
        for k, (src, dst) in enumerate(
            [
                (clip_hbm, clip_ref),
                (w_hbm, tab.at[pl.ds(0, TAPS)]),
                (w_in_hbm, w_in_ref),
                (b_hbm, b_ref),
                (lat_hbm, latx.at[pl.ds(HALO, slab)]),
                (hid_hbm, hid),
                (fw_hbm, fw_ref),
                (modu_hbm, modu_ref),
                (lat_hbm, lat_own),
            ]
        )
    ]
    own_clip, own_w, own_w_in, own_b, own_lat, own_hid, own_fw, own_modu, own_lat2 = loads
    own_g = [pltpu.make_async_copy(grad_hbm.at[t], g.at[t], s_g_in.at[t]) for t in range(slab)]
    for c in [own_w_in, own_b, own_lat2, own_clip, own_w] + own_g + [own_lat, own_fw, own_modu, own_hid]:
        c.start()

    barrier = pltpu.get_barrier_semaphore()
    greeted = [(p * CORES + core, j) for _, p in tms] + [sibling] + [(i, p) for _, p in seqs]
    greeted += [(lax.rem(i + 1, n_tm), p) for p in range(n_seq)] + [(lax.rem(i + n_tm - 1, n_tm), j)]
    for to in greeted:
        pl.semaphore_signal(barrier, inc=1, device_id=to, device_id_type=MESH)

    def copy(src, dst, send, recv, to):
        return pltpu.make_async_remote_copy(
            src_ref=src, dst_ref=dst, send_sem=send, recv_sem=recv, device_id=to, device_id_type=MESH
        )

    def lat_copy(to):
        return copy(lat_hbm.at[pl.ds(slab - HALO, HALO)], latx.at[pl.ds(0, HALO)], s_lat, r_lat, (to, j))

    def clip_of(frame):
        return clip_ref[jnp.clip(frame, 0, frames - 1)]

    def source(frame, tap):
        return jnp.maximum(frame - tap, clip_of(frame))

    n = width // PATCH
    e = cl * PATCH
    row = lax.broadcasted_iota(jnp.int32, (width, width), 0)
    col = lax.broadcasted_iota(jnp.int32, (width, width), 1)
    spread[...] = jnp.where(row == lax.rem(col, n) * PATCH + lax.div(col, n), 1.0, 0.0).astype(BF16)
    row = lax.broadcasted_iota(jnp.int32, (e, e), 0)
    col = lax.broadcasted_iota(jnp.int32, (e, e), 1)
    order = jnp.where(row == lax.rem(col, cl) * PATCH + lax.div(col, cl), 1.0, 0.0).astype(BF16)
    def prepare(r, held, base):
        frame = first + r - 2
        for tap in range(TAPS):
            row = jnp.clip(source(frame, tap) - base, 0, held.shape[0] - 1)
            z[r, tap * cl : (tap + 1) * cl] = held[row]
        z[r, TAPS * cl :] = jnp.ones((cl, width), BF16)
        pre = dot(w64[...], z[r], 1, 0)
        sig = sigmoid(pre)
        a = pre * sig
        act[r] = a.astype(BF16)
        return sig + a * (1.0 - sig)

    own_w_in.wait()
    own_b.wait()
    load_in_weights(w_in_ref, b_ref, w64)
    own_clip.wait()
    own_lat2.wait()
    for r in range(HALO, slab + 2):
        slope[r - HALO] = prepare(r, lat_own, first)
    own_w.wait()
    later = tab[1].astype(F32) + tab[2].astype(F32)
    tab[TAPS] = later.astype(BF16)
    tab[TAPS + 1] = (later + tab[0].astype(F32)).astype(BF16)
    tab[TAPS + 2] = jnp.zeros_like(tab[TAPS + 2])

    def choice(t, back):
        start = clip_of(first + t)
        back1 = start < first + t
        back2 = start < first + t - 1
        if back == 0:
            return jnp.where(back1, 0, TAPS + 1)
        if back == 1:
            return jnp.where(back2, 1, jnp.where(back1, TAPS, TAPS + 2))
        return jnp.where(back2, 2, TAPS + 2)

    def grad_act(r):
        ga[r] = sum(
            dot(tab[choice(r - 2 + back, back)], g[r - 2 + back], 0, 0)
            for back in range(TAPS)
            if 0 <= r - 2 + back < slab
        )

    own_g[0].wait()
    grad_act(0)
    own_g[1].wait()
    grad_act(1)
    pl.semaphore_wait(barrier, len(greeted))

    @pl.when(i < n_tm - 1)
    def _():
        lat_copy(i + 1).start()

    @pl.when(i == 0)
    def _():
        latx[0:HALO] = jnp.zeros_like(latx[0:HALO])

    for r in range(2, slab + 2):
        if r < slab:
            own_g[r].wait()
        grad_act(r)

    own_lat.wait()

    @pl.when(i < n_tm - 1)
    def _():
        lat_copy(i + 1).wait_send()

    @pl.when(i > 0)
    def _():
        lat_copy(i).wait_recv()

    def finish(r):
        factor = prepare(r, latx, first - HALO) if r < HALO else slope[r - HALO]
        grad_pre = (ga[r] * factor).astype(BF16)
        gp[r] = grad_pre
        parts[r] = dot(w_in_ref[...], grad_pre, 1, 0)

    def scatter(r):
        start = clip_of(first + r - 2)
        back1 = jnp.where(start < first + r - 2, 1.0, 0.0).astype(F32)
        back2 = jnp.where(start < first + r - 3, 1.0, 0.0).astype(F32)
        p0, p1, p2 = [parts[r, tap * cl : (tap + 1) * cl] for tap in range(TAPS)]
        lg[r + 2] += p0 + (1.0 - back1) * (p1 + p2)
        lg[r + 1] += back1 * p1 + (back1 - back2) * p2
        lg[r] += back2 * p2

    lg[...] = jnp.zeros_like(lg)
    for r in range(HALO):
        finish(r)
    for r in range(HALO):
        scatter(r)
    lgh[...] = lg[0:HALO].astype(BF16)

    def halo_copy(to, p):
        return copy(lgh.at[p], tokh.at[j], s_halo.at[p], r_halo.at[j], (to, p))

    @pl.when(i > 0)
    def _():
        for p in range(n_seq):
            halo_copy(i - 1, p).start()

    @pl.when(i == n_tm - 1)
    def _():
        tokh[...] = jnp.zeros_like(tokh)

    for r in range(HALO, slab + 2):
        finish(r)
    for r in range(HALO, slab + 2):
        scatter(r)
    lgs[...] = lg[HALO : HALO + slab].astype(BF16)
    tok_copies = [copy(lgs.at[p], tok.at[j], s_tok.at[d - 1], r_tok.at[d - 1], (i, p)) for d, p in seqs]
    for c in tok_copies:
        c.start()

    rows = chans // (n_tm * n_seq)
    block = n_seq * rows

    def weight(tap):
        total = sum(
            dot(g[t], act[jnp.clip(source(first + t, tap) - first + 2, 0, slab + 1)], 1, 1) for t in range(slab)
        )
        for q in range(chips):
            for c in range(CORES):
                at = (q * CORES + c) * block
                w4[tap, c, q] = total[at : at + block].astype(BF16)

    w_core = [
        copy(w4.at[tap, other], wcore.at[tap], s_wc.at[tap], r_wc.at[tap], sibling) for tap in range(TAPS)
    ]
    w_xy = [
        [
            copy(whalf.at[tap, p], wrecv.at[tap, d - 1], s_w.at[tap, d - 1], r_w.at[tap, d - 1], (p * CORES + core, j))
            for d, p in tms
        ]
        for tap in range(TAPS)
    ]
    w_z = [
        [
            copy(wsum.at[tap, p], wrecv2.at[tap, d - 1], s_w2.at[tap, d - 1], r_w2.at[tap, d - 1], (i, p))
            for d, p in seqs
        ]
        for tap in range(TAPS)
    ]

    def weight_xy(tap):
        w_core[tap].wait()
        whalf[tap] = (w4[tap, core].astype(F32) + wcore[tap].astype(F32)).astype(BF16)
        for c in w_xy[tap]:
            c.start()

    def weight_z(tap):
        for c in w_xy[tap]:
            c.wait()
        total = whalf[tap, chip].astype(F32)
        for k in range(chips - 1):
            total = total + wrecv[tap, k].astype(F32)
        for p in range(n_seq):
            wsum[tap, p] = total[p * rows : (p + 1) * rows].astype(BF16)
        for c in w_z[tap]:
            c.start()

    def weight_end(tap):
        for c in w_z[tap]:
            c.wait()
        total = wsum[tap, j].astype(F32)
        for k in range(n_seq - 1):
            total = total + wrecv2[tap, k].astype(F32)
        wg_ref[tap] = total

    weight(0)
    w_core[0].start()
    own_hid.wait()
    step_rows = 128

    @pl.loop(0, hid.shape[0] // step_rows)
    def _(r):
        at = pl.ds(pl.multiple_of(r * step_rows, step_rows), step_rows)
        h = hid[at, :].astype(F32)
        center = h - jnp.mean(h, axis=1, keepdims=True)
        scaled = lax.rsqrt(jnp.mean(center * center, axis=1, keepdims=True) + 1e-06)
        nb[at, :] = (center * scaled).astype(BF16)
        inv[at, :] = jnp.broadcast_to(scaled, (step_rows, inv.shape[1]))

    weight_xy(0)
    weight(1)
    w_core[1].start()
    misc[...] = sum(dot(z[r], gp[r], 1, 1) for r in range(slab + 2))
    weight_xy(1)

    own_fw.wait()
    own_modu.wait()
    shift = modu_ref[0:1, :]
    scale = 1.0 + modu_ref[1:2, :]

    @pl.when(i > 0)
    def _():
        for p in range(n_seq):
            halo_copy(i - 1, p).wait_send()

    @pl.when(i < n_tm - 1)
    def _():
        for p in range(n_seq):
            copy(lgh.at[0], tokh.at[p], s_halo.at[0], r_halo.at[p], (i, j)).wait_recv()

    for c in tok_copies:
        c.wait()
    tok[j] = lgs[j]

    lat = jnp.concatenate([(tok[r].astype(F32) + tokh[r].astype(F32)).astype(BF16) for r in range(n_seq)], axis=0)
    split = dot(lat, spread[...], 1, 0)
    stack = jnp.concatenate(
        [
            jnp.concatenate([split[r * cl : (r + 1) * cl, q * n : (q + 1) * n] for r in range(n_seq)], axis=1)
            for q in range(PATCH)
        ],
        axis=0,
    )
    tg_t = dot(order, stack.astype(BF16), 1, 0)
    facc[...] = dot(tg_t.astype(BF16), nb[...], 1, 0)
    column = jnp.sum(tg_t, axis=1, keepdims=True)
    tgs[...] = tg_t.T.astype(BF16)

    fw = fw_ref[...].astype(F32)
    macc[0:1] = jnp.sum(fw * column, axis=0, keepdims=True)
    macc[1:2] = jnp.sum(fw * facc[...], axis=0, keepdims=True)
    facc[...] = facc[...] * scale + column * shift

    pieces = d_model // chans
    small = jnp.concatenate(
        [misc[0 : TAPS * cl + 1, :]]
        + [macc[b : b + 1, p * chans : (p + 1) * chans] for b in range(2) for p in range(pieces)]
        + [jnp.zeros((e - TAPS * cl - 1 - 2 * pieces, chans), F32)],
        axis=0,
    )
    nc, er, cwc = f4.shape[0], f4.shape[3], f4.shape[4]
    for a, c, k, lo, mid, end in places(n_tm, e // er, nc, cwc, d_model, chans):
        at = slice(k * er, (k + 1) * er)
        to = f4.at[c, a % CORES, a // CORES]
        if mid > lo:
            to[:, : mid - lo] = facc[at, lo:mid].astype(BF16)
        if end > mid:
            to[:, mid - lo : end - lo] = small[at, mid - d_model : end - d_model].astype(BF16)
        if lo + cwc > end:
            to[:, end - lo :] = jnp.zeros((er, lo + cwc - end), BF16)
    chunks = range(nc)
    f_core = [copy(f4.at[c, other], fcore.at[c], s_fc.at[c], r_fc.at[c], sibling) for c in chunks]
    for c in chunks:
        f_core[c].start()

    half = hid.shape[0] // 2

    def input_gradient(k):
        at = slice(k * half, (k + 1) * half)
        normed = nb[at, :].astype(F32)
        ng = dot(tgs[at, :], fw_ref[...], 1, 0) * scale
        m1 = jnp.mean(ng, axis=1, keepdims=True)
        m2 = jnp.mean(ng * normed, axis=1, keepdims=True)
        dx_ref[at, :] = (inv[at, 0:1] * (ng - m1 - normed * m2)).astype(BF16)

    f_xy = [
        [
            copy(fhalf.at[c, p], frecv.at[c, d - 1], s_f.at[c, d - 1], r_f.at[c, d - 1], (p * CORES + core, j))
            for d, p in tms
        ]
        for c in chunks
    ]
    f_z = [
        [copy(fall.at[c, j], fall.at[c, j], s_f2.at[c, d - 1], r_f2.at[c, d - 1], (i, p)) for d, p in seqs]
        for c in chunks
    ]
    g_xy = [
        [
            copy(
                gath.at[c, core, chip], gath.at[c, core, chip], s_g.at[c, d - 1], r_g.at[c, d - 1],
                (p * CORES + core, j),
            )
            for d, p in tms
        ]
        for c in chunks
    ]
    g_core = [copy(gath.at[c, core], gath.at[c, core], s_gc.at[c], r_gc.at[c], sibling) for c in chunks]

    def start(copies):
        for c in copies:
            c.start()

    def wait(copies):
        for c in copies:
            c.wait()

    def final_xy(c):
        f_core[c].wait()
        for q in range(chips):
            fhalf[c, q] = (f4[c, core, q].astype(F32) + fcore[c, q].astype(F32)).astype(BF16)
        start(f_xy[c])

    def final_z(c):
        wait(f_xy[c])
        total = fhalf[c, chip].astype(F32)
        for k in range(chips - 1):
            total = total + frecv[c, k].astype(F32)
        fall[c, j] = total.astype(BF16)
        start(f_z[c])

    def gather_xy(c):
        wait(f_z[c])
        total = fall[c, 0].astype(F32)
        for k in range(1, n_seq):
            total = total + fall[c, k].astype(F32)
        gath[c, core, chip] = total.astype(BF16)
        start(g_xy[c])

    def gather_core(c):
        wait(g_xy[c])
        g_core[c].start()

    weight(2)
    w_core[2].start()
    for c in chunks:
        final_xy(c)
    weight_z(0)
    input_gradient(0)
    weight_z(1)
    input_gradient(1)
    for c in chunks:
        final_z(c)
    weight_xy(2)
    weight_end(0)
    weight_end(1)
    for c in chunks:
        gather_xy(c)
    weight_z(2)
    for c in chunks:
        gather_core(c)
    weight_end(2)
    wait(g_core)


def unpack_kernel(gath, wg_ref, dx_in, fin_ref, mod_ref, in_ref, bias_ref, wg_out, dx_hbm, small, sem):
    part = dx_in.shape[0] // sem.shape[0]
    dx_copies = [
        pltpu.make_async_copy(dx_in.at[pl.ds(k * part, part)], dx_hbm.at[pl.ds(k * part, part)], sem.at[k])
        for k in range(sem.shape[0])
    ]
    for c in dx_copies:
        c.start()
    nc, cores, chips, er, cwc = gath.shape
    n_tm = cores * chips
    d_model = fin_ref.shape[1]
    taps_cl, chans = in_ref.shape
    pieces = d_model // chans
    for a, c, k, lo, mid, end in places(n_tm, fin_ref.shape[0] // er, nc, cwc, d_model, chans):
        at = slice(k * er, (k + 1) * er)
        part = gath.at[c, a % cores, a // cores]
        if mid > lo:
            fin_ref[at, lo:mid] = part[:, : mid - lo].astype(F32)
        if end > mid:
            small[at, mid - d_model : end - d_model] = part[:, mid - lo : end - lo].astype(F32)
    in_ref[...] = small[:taps_cl, :]
    bias_ref[...] = small[taps_cl : taps_cl + 1, :]
    for b in range(2):
        for p in range(pieces):
            at = taps_cl + 1 + b * pieces + p
            mod_ref[b : b + 1, p * chans : (p + 1) * chans] = small[at : at + 1, :]
    wg_out[...] = wg_ref[...]
    for c in dx_copies:
        c.wait()


def local(n_tm, n_seq, latents, hidden, grad_out, conv_in_w, conv_in_b, conv_w, final_w, modulation, clip_start):
    slab, cl, width = latents.shape
    taps, chans = conv_w.shape[:2]
    tokens, d_model = hidden.shape
    rows = chans // (n_tm * n_seq)
    block = n_seq * rows
    chips = n_tm // CORES
    w_in = conv_in_w.transpose(0, 2, 1).reshape(taps * cl, chans)
    bias = conv_in_b.reshape(1, chans)
    e = cl * PATCH
    er = 16
    parts = n_tm // (e // er)
    lanes = -(-(d_model + chans) // (parts * 128))
    nc = max(c for c in range(1, CHUNKS + 1) if lanes % c == 0)
    cw = lanes // nc * 128
    vmem = pl.BlockSpec(memory_space=pltpu.VMEM)
    hbm = pl.BlockSpec(memory_space=pltpu.HBM)
    smem = pl.BlockSpec(memory_space=pltpu.SMEM)
    dma = pltpu.SemaphoreType.DMA
    nt, ns = chips - 1, n_seq - 1

    def b16(*shape):
        return pltpu.VMEM(shape, BF16)

    def f32(*shape):
        return pltpu.VMEM(shape, F32)

    def in_hbm(x):
        return pltpu.with_memory_space_constraint(x, pltpu.HBM)

    dx, wg, gath = pl.pallas_call(
        functools.partial(main_kernel, n_tm, n_seq),
        out_shape=(
            b16(tokens, d_model),
            f32(taps, rows, chans),
            b16(nc, CORES, chips, er, cw),
        ),
        in_specs=[hbm] * 9,
        out_specs=(vmem, vmem, vmem),
        scratch_shapes=[
            pltpu.SMEM(clip_start.shape, jnp.int32),
            b16(taps * cl, chans),
            f32(1, chans),
            b16(e, d_model),
            f32(2, d_model),
            b16(slab + HALO, cl, width),
            b16(slab, cl, width),
            f32(slab + 2 - HALO, chans, width),
            b16(slab, chans, width),
            b16(tokens, d_model),
            b16(tokens, d_model),
            f32(tokens, 128),
            b16(chans, 4 * cl),
            b16(slab + 2, 4 * cl, width),
            b16(taps + 3, chans, chans),
            b16(slab + 2, chans, width),
            f32(slab + 2, chans, width),
            b16(slab + 2, chans, width),
            f32(slab + 2, taps * cl, width),
            f32(4 * cl, chans),
            f32(slab + HALO, cl, width),
            b16(HALO, cl, width),
            b16(slab, cl, width),
            b16(n_seq, cl, width),
            b16(n_seq, cl, width),
            b16(taps, CORES, chips, block, chans),
            b16(taps, chips, block, chans),
            b16(taps, chips, block, chans),
            b16(taps, nt, block, chans),
            b16(taps, n_seq, rows, chans),
            b16(taps, ns, rows, chans),
            b16(width, width),
            b16(tokens, e),
            f32(e, d_model),
            f32(8, d_model),
            b16(nc, CORES, chips, er, cw),
            b16(nc, chips, er, cw),
            b16(nc, chips, er, cw),
            b16(nc, nt, er, cw),
            b16(nc, n_seq, er, cw),
            dma((9,)), dma((slab,)), dma(()), dma(()), dma((n_seq,)), dma((n_seq,)), dma((ns,)), dma((ns,)),
            dma((taps,)), dma((taps,)), dma((taps, nt)), dma((taps, nt)), dma((taps, ns)), dma((taps, ns)),
            dma((nc,)), dma((nc,)), dma((nc, nt)), dma((nc, nt)), dma((nc, ns)), dma((nc, ns)),
            dma((nc, nt)), dma((nc, nt)), dma((nc,)), dma((nc,)),
        ],
        compiler_params=pltpu.CompilerParams(
            vmem_limit_bytes=MAIN_VMEM, collective_id=0, has_side_effects=True
        ),
        name="main",
    )(*[in_hbm(x) for x in (clip_start, latents, hidden, grad_out, w_in, bias, conv_w, final_w.T, modulation)])
    fin, mod, w_in_grad, bias_grad, wg, dx = pl.pallas_call(
        unpack_kernel,
        out_shape=(
            jax.ShapeDtypeStruct((e, d_model), F32),
            jax.ShapeDtypeStruct((2, d_model), F32),
            jax.ShapeDtypeStruct((taps * cl, chans), F32),
            jax.ShapeDtypeStruct((1, chans), F32),
            jax.ShapeDtypeStruct((taps, rows, chans), F32),
            jax.ShapeDtypeStruct((tokens, d_model), BF16),
        ),
        in_specs=[vmem, vmem, vmem],
        out_specs=(vmem,) * 5 + (hbm,),
        scratch_shapes=[f32(e, chans), dma((4,))],
        compiler_params=pltpu.CompilerParams(vmem_limit_bytes=SMALL_VMEM),
        name="unpack",
    )(gath, wg, dx)
    return (
        dx,
        wg.transpose(1, 0, 2),
        w_in_grad.reshape(taps, cl, chans).transpose(0, 2, 1),
        bias_grad.reshape(chans),
        fin.T,
        mod,
    )


def solution(mesh):
    return jax.shard_map(
        functools.partial(local, mesh.shape["tm"], mesh.shape["seq"]),
        mesh=mesh,
        in_specs=(
            P("tm", None, "seq"),
            P(("tm", "seq"), None),
            P("tm", None, "seq"),
            P(),
            P(),
            P(),
            P(),
            P(),
            P(),
        ),
        out_specs=(P(("tm", "seq"), None), P(("tm", "seq"), None, None), P(), P(), P(), P()),
        check_vma=False,
    )
```

```python
import functools

import jax
import jax.numpy as jnp
from jax import lax
from jax.experimental import pallas as pl
from jax.experimental.pallas import tpu as pltpu
from jax.sharding import PartitionSpec as P

F32 = jnp.float32
BF16 = jnp.bfloat16
MESH = pl.DeviceIdType.MESH
PATCH = 4
CORES = 2
TAPS = 3
HALO = 4
CHUNKS = 2
MAIN_VMEM = 46 * 1024 * 1024
SMALL_VMEM = 12 * 1024 * 1024


def dot(a, b, ca, cb):
    return lax.dot_general(a, b, (((ca,), (cb,)), ((), ())), preferred_element_type=F32)


def load_in_weights(w_in_ref, b_ref, w64):
    bias = b_ref[...]
    hi = bias.astype(BF16)
    mid = (bias - hi.astype(F32)).astype(BF16)
    lo = (bias - hi.astype(F32) - mid.astype(F32)).astype(BF16)
    pad = jnp.zeros((16 - 3, bias.shape[1]), F32)
    rows = jnp.concatenate(
        [w_in_ref[...].astype(F32), hi.astype(F32), mid.astype(F32), lo.astype(F32), pad], axis=0
    )
    w64[...] = rows.T.astype(BF16)


def places(n_tm, groups, nc, width, wide, narrow):
    parts = n_tm // groups
    for a in range(n_tm):
        for c in range(nc):
            lo = ((a % parts) * nc + c) * width
            mid = min(max(lo, wide), lo + width)
            end = min(max(lo, wide + narrow), lo + width)
            yield a, c, a // parts, lo, mid, end


def sigmoid(x):
    return 0.5 * jnp.tanh(0.5 * x) + 0.5


def main_kernel(
    n_tm, n_seq,
    clip_hbm, lat_hbm, hid_hbm, grad_hbm, w_in_hbm, b_hbm, w_hbm, fw_hbm, modu_hbm,
    dx_ref, wg_ref, gath,
    clip_ref, w_in_ref, b_ref, fw_ref, modu_ref,
    latx, lat_own, slope, g, hid, nb, inv, w64, z, tab, act, ga, gp, parts, misc, lg, lgh, lgs, tok, tokh,
    w4, wcore, whalf, wrecv, wsum, wrecv2,
    spread, tgs, facc, macc, f4, fcore, fhalf, frecv, fall,
    s_in, s_g_in, s_lat, r_lat, s_halo, r_halo, s_tok, r_tok,
    s_wc, r_wc, s_w, r_w, s_w2, r_w2,
    s_fc, r_fc, s_f, r_f, s_f2, r_f2, s_g, r_g, s_gc, r_gc,
):
    i = lax.axis_index("tm")
    j = lax.axis_index("seq")
    chips = n_tm // CORES
    core = lax.rem(i, CORES)
    chip = lax.div(i, CORES)
    other = CORES - 1 - core
    sibling = (chip * CORES + other, j)
    tms = [(d, lax.rem(chip + d, chips)) for d in range(1, chips)]
    seqs = [(d, lax.rem(j + d, n_seq)) for d in range(1, n_seq)]
    slab, chans = g.shape[:2]
    cl, width = latx.shape[1:]
    frames = clip_ref.shape[0]
    d_model = hid.shape[1]
    first = i * slab

    loads = [
        pltpu.make_async_copy(src, dst, s_in.at[k])
        for k, (src, dst) in enumerate(
            [
                (clip_hbm, clip_ref),
                (w_hbm, tab.at[pl.ds(0, TAPS)]),
                (w_in_hbm, w_in_ref),
                (b_hbm, b_ref),
                (lat_hbm, latx.at[pl.ds(HALO, slab)]),
                (hid_hbm, hid),
                (fw_hbm, fw_ref),
                (modu_hbm, modu_ref),
                (lat_hbm, lat_own),
            ]
        )
    ]
    own_clip, own_w, own_w_in, own_b, own_lat, own_hid, own_fw, own_modu, own_lat2 = loads
    own_g = [pltpu.make_async_copy(grad_hbm.at[t], g.at[t], s_g_in.at[t]) for t in range(slab)]
    for c in [own_w_in, own_b, own_lat2, own_clip, own_w] + own_g + [own_lat, own_fw, own_modu, own_hid]:
        c.start()

    barrier = pltpu.get_barrier_semaphore()
    greeted = [(p * CORES + core, j) for _, p in tms] + [sibling] + [(i, p) for _, p in seqs]
    greeted += [(lax.rem(i + 1, n_tm), p) for p in range(n_seq)] + [(lax.rem(i + n_tm - 1, n_tm), j)]
    for to in greeted:
        pl.semaphore_signal(barrier, inc=1, device_id=to, device_id_type=MESH)

    def copy(src, dst, send, recv, to):
        return pltpu.make_async_remote_copy(
            src_ref=src, dst_ref=dst, send_sem=send, recv_sem=recv, device_id=to, device_id_type=MESH
        )

    def lat_copy(to):
        return copy(lat_hbm.at[pl.ds(slab - HALO, HALO)], latx.at[pl.ds(0, HALO)], s_lat, r_lat, (to, j))

    def clip_of(frame):
        return clip_ref[jnp.clip(frame, 0, frames - 1)]

    def source(frame, tap):
        return jnp.maximum(frame - tap, clip_of(frame))

    n = width // PATCH
    e = cl * PATCH
    row = lax.broadcasted_iota(jnp.int32, (width, width), 0)
    col = lax.broadcasted_iota(jnp.int32, (width, width), 1)
    spread[...] = jnp.where(row == lax.rem(col, n) * PATCH + lax.div(col, n), 1.0, 0.0).astype(BF16)
    row = lax.broadcasted_iota(jnp.int32, (e, e), 0)
    col = lax.broadcasted_iota(jnp.int32, (e, e), 1)
    order = jnp.where(row == lax.rem(col, cl) * PATCH + lax.div(col, cl), 1.0, 0.0).astype(BF16)
    def prepare(r, held, base):
        frame = first + r - 2
        for tap in range(TAPS):
            row = jnp.clip(source(frame, tap) - base, 0, held.shape[0] - 1)
            z[r, tap * cl : (tap + 1) * cl] = held[row]
        z[r, TAPS * cl :] = jnp.ones((cl, width), BF16)
        pre = dot(w64[...], z[r], 1, 0)
        sig = sigmoid(pre)
        a = pre * sig
        act[r] = a.astype(BF16)
        return sig + a * (1.0 - sig)

    own_w_in.wait()
    own_b.wait()
    load_in_weights(w_in_ref, b_ref, w64)
    own_clip.wait()
    own_lat2.wait()
    for r in range(HALO, slab + 2):
        slope[r - HALO] = prepare(r, lat_own, first)
    own_w.wait()
    later = tab[1].astype(F32) + tab[2].astype(F32)
    tab[TAPS] = later.astype(BF16)
    tab[TAPS + 1] = (later + tab[0].astype(F32)).astype(BF16)
    tab[TAPS + 2] = jnp.zeros_like(tab[TAPS + 2])

    def choice(t, back):
        start = clip_of(first + t)
        back1 = start < first + t
        back2 = start < first + t - 1
        if back == 0:
            return jnp.where(back1, 0, TAPS + 1)
        if back == 1:
            return jnp.where(back2, 1, jnp.where(back1, TAPS, TAPS + 2))
        return jnp.where(back2, 2, TAPS + 2)

    def grad_act(r):
        ga[r] = sum(
            dot(tab[choice(r - 2 + back, back)], g[r - 2 + back], 0, 0)
            for back in range(TAPS)
            if 0 <= r - 2 + back < slab
        )

    own_g[0].wait()
    grad_act(0)
    own_g[1].wait()
    grad_act(1)
    pl.semaphore_wait(barrier, len(greeted))

    @pl.when(i < n_tm - 1)
    def _():
        lat_copy(i + 1).start()

    @pl.when(i == 0)
    def _():
        latx[0:HALO] = jnp.zeros_like(latx[0:HALO])

    for r in range(2, slab + 2):
        if r < slab:
            own_g[r].wait()
        grad_act(r)

    own_lat.wait()

    @pl.when(i < n_tm - 1)
    def _():
        lat_copy(i + 1).wait_send()

    @pl.when(i > 0)
    def _():
        lat_copy(i).wait_recv()

    def finish(r):
        factor = prepare(r, latx, first - HALO) if r < HALO else slope[r - HALO]
        grad_pre = (ga[r] * factor).astype(BF16)
        gp[r] = grad_pre
        parts[r] = dot(w_in_ref[...], grad_pre, 1, 0)

    def scatter(r):
        start = clip_of(first + r - 2)
        back1 = jnp.where(start < first + r - 2, 1.0, 0.0).astype(F32)
        back2 = jnp.where(start < first + r - 3, 1.0, 0.0).astype(F32)
        p0, p1, p2 = [parts[r, tap * cl : (tap + 1) * cl] for tap in range(TAPS)]
        lg[r + 2] += p0 + (1.0 - back1) * (p1 + p2)
        lg[r + 1] += back1 * p1 + (back1 - back2) * p2
        lg[r] += back2 * p2

    lg[...] = jnp.zeros_like(lg)
    for r in range(HALO):
        finish(r)
    for r in range(HALO):
        scatter(r)
    lgh[...] = lg[0:HALO].astype(BF16)

    def halo_copy(to, p):
        return copy(lgh.at[p], tokh.at[j], s_halo.at[p], r_halo.at[j], (to, p))

    @pl.when(i > 0)
    def _():
        for p in range(n_seq):
            halo_copy(i - 1, p).start()

    @pl.when(i == n_tm - 1)
    def _():
        tokh[...] = jnp.zeros_like(tokh)

    for r in range(HALO, slab + 2):
        finish(r)
    for r in range(HALO, slab + 2):
        scatter(r)
    lgs[...] = lg[HALO : HALO + slab].astype(BF16)
    tok_copies = [copy(lgs.at[p], tok.at[j], s_tok.at[d - 1], r_tok.at[d - 1], (i, p)) for d, p in seqs]
    for c in tok_copies:
        c.start()

    rows = chans // (n_tm * n_seq)
    block = n_seq * rows

    def weight(tap):
        total = sum(
            dot(g[t], act[jnp.clip(source(first + t, tap) - first + 2, 0, slab + 1)], 1, 1) for t in range(slab)
        )
        for q in range(chips):
            for c in range(CORES):
                at = (q * CORES + c) * block
                w4[tap, c, q] = total[at : at + block].astype(BF16)

    w_core = [
        copy(w4.at[tap, other], wcore.at[tap], s_wc.at[tap], r_wc.at[tap], sibling) for tap in range(TAPS)
    ]
    w_xy = [
        [
            copy(whalf.at[tap, p], wrecv.at[tap, d - 1], s_w.at[tap, d - 1], r_w.at[tap, d - 1], (p * CORES + core, j))
            for d, p in tms
        ]
        for tap in range(TAPS)
    ]
    w_z = [
        [
            copy(wsum.at[tap, p], wrecv2.at[tap, d - 1], s_w2.at[tap, d - 1], r_w2.at[tap, d - 1], (i, p))
            for d, p in seqs
        ]
        for tap in range(TAPS)
    ]

    def weight_xy(tap):
        w_core[tap].wait()
        whalf[tap] = (w4[tap, core].astype(F32) + wcore[tap].astype(F32)).astype(BF16)
        for c in w_xy[tap]:
            c.start()

    def weight_z(tap):
        for c in w_xy[tap]:
            c.wait()
        total = whalf[tap, chip].astype(F32)
        for k in range(chips - 1):
            total = total + wrecv[tap, k].astype(F32)
        for p in range(n_seq):
            wsum[tap, p] = total[p * rows : (p + 1) * rows].astype(BF16)
        for c in w_z[tap]:
            c.start()

    def weight_end(tap):
        for c in w_z[tap]:
            c.wait()
        total = wsum[tap, j].astype(F32)
        for k in range(n_seq - 1):
            total = total + wrecv2[tap, k].astype(F32)
        wg_ref[tap] = total

    weight(0)
    w_core[0].start()
    weight(1)
    w_core[1].start()
    weight_xy(0)
    own_hid.wait()
    step_rows = 128

    @pl.loop(0, hid.shape[0] // step_rows)
    def _(r):
        at = pl.ds(pl.multiple_of(r * step_rows, step_rows), step_rows)
        h = hid[at, :].astype(F32)
        center = h - jnp.mean(h, axis=1, keepdims=True)
        scaled = lax.rsqrt(jnp.mean(center * center, axis=1, keepdims=True) + 1e-06)
        nb[at, :] = (center * scaled).astype(BF16)
        inv[at, :] = jnp.broadcast_to(scaled, (step_rows, inv.shape[1]))

    weight_xy(1)
    misc[...] = sum(dot(z[r], gp[r], 1, 1) for r in range(slab + 2))

    own_fw.wait()
    own_modu.wait()
    shift = modu_ref[0:1, :]
    scale = 1.0 + modu_ref[1:2, :]

    @pl.when(i > 0)
    def _():
        for p in range(n_seq):
            halo_copy(i - 1, p).wait_send()

    @pl.when(i < n_tm - 1)
    def _():
        for p in range(n_seq):
            copy(lgh.at[0], tokh.at[p], s_halo.at[0], r_halo.at[p], (i, j)).wait_recv()

    for c in tok_copies:
        c.wait()
    tok[j] = lgs[j]

    lat = jnp.concatenate([(tok[r].astype(F32) + tokh[r].astype(F32)).astype(BF16) for r in range(n_seq)], axis=0)
    split = dot(lat, spread[...], 1, 0)
    stack = jnp.concatenate(
        [
            jnp.concatenate([split[r * cl : (r + 1) * cl, q * n : (q + 1) * n] for r in range(n_seq)], axis=1)
            for q in range(PATCH)
        ],
        axis=0,
    )
    tg_t = dot(order, stack.astype(BF16), 1, 0)
    facc[...] = dot(tg_t.astype(BF16), nb[...], 1, 0)
    column = jnp.sum(tg_t, axis=1, keepdims=True)
    tgs[...] = tg_t.T.astype(BF16)

    fw = fw_ref[...].astype(F32)
    macc[0:1] = jnp.sum(fw * column, axis=0, keepdims=True)
    macc[1:2] = jnp.sum(fw * facc[...], axis=0, keepdims=True)
    facc[...] = facc[...] * scale + column * shift

    pieces = d_model // chans
    small = jnp.concatenate(
        [misc[0 : TAPS * cl + 1, :]]
        + [macc[b : b + 1, p * chans : (p + 1) * chans] for b in range(2) for p in range(pieces)]
        + [jnp.zeros((e - TAPS * cl - 1 - 2 * pieces, chans), F32)],
        axis=0,
    )
    nc, er, cwc = f4.shape[0], f4.shape[3], f4.shape[4]
    for a, c, k, lo, mid, end in places(n_tm, e // er, nc, cwc, d_model, chans):
        at = slice(k * er, (k + 1) * er)
        to = f4.at[c, a % CORES, a // CORES]
        if mid > lo:
            to[:, : mid - lo] = facc[at, lo:mid].astype(BF16)
        if end > mid:
            to[:, mid - lo : end - lo] = small[at, mid - d_model : end - d_model].astype(BF16)
        if lo + cwc > end:
            to[:, end - lo :] = jnp.zeros((er, lo + cwc - end), BF16)
    chunks = range(nc)
    f_core = [copy(f4.at[c, other], fcore.at[c], s_fc.at[c], r_fc.at[c], sibling) for c in chunks]
    for c in chunks:
        f_core[c].start()

    half = hid.shape[0] // 2

    def input_gradient(k):
        at = slice(k * half, (k + 1) * half)
        normed = nb[at, :].astype(F32)
        ng = dot(tgs[at, :], fw_ref[...], 1, 0) * scale
        m1 = jnp.mean(ng, axis=1, keepdims=True)
        m2 = jnp.mean(ng * normed, axis=1, keepdims=True)
        dx_ref[at, :] = (inv[at, 0:1] * (ng - m1 - normed * m2)).astype(BF16)

    f_xy = [
        [
            copy(fhalf.at[c, p], frecv.at[c, d - 1], s_f.at[c, d - 1], r_f.at[c, d - 1], (p * CORES + core, j))
            for d, p in tms
        ]
        for c in chunks
    ]
    f_z = [
        [copy(fall.at[c, j], fall.at[c, j], s_f2.at[c, d - 1], r_f2.at[c, d - 1], (i, p)) for d, p in seqs]
        for c in chunks
    ]
    g_xy = [
        [
            copy(
                gath.at[c, core, chip], gath.at[c, core, chip], s_g.at[c, d - 1], r_g.at[c, d - 1],
                (p * CORES + core, j),
            )
            for d, p in tms
        ]
        for c in chunks
    ]
    g_core = [copy(gath.at[c, core], gath.at[c, core], s_gc.at[c], r_gc.at[c], sibling) for c in chunks]

    def start(copies):
        for c in copies:
            c.start()

    def wait(copies):
        for c in copies:
            c.wait()

    def final_xy(c):
        f_core[c].wait()
        for q in range(chips):
            fhalf[c, q] = (f4[c, core, q].astype(F32) + fcore[c, q].astype(F32)).astype(BF16)
        start(f_xy[c])

    def final_z(c):
        wait(f_xy[c])
        total = fhalf[c, chip].astype(F32)
        for k in range(chips - 1):
            total = total + frecv[c, k].astype(F32)
        fall[c, j] = total.astype(BF16)
        start(f_z[c])

    def gather_xy(c):
        wait(f_z[c])
        total = fall[c, 0].astype(F32)
        for k in range(1, n_seq):
            total = total + fall[c, k].astype(F32)
        gath[c, core, chip] = total.astype(BF16)
        start(g_xy[c])

    def gather_core(c):
        wait(g_xy[c])
        g_core[c].start()

    weight(2)
    w_core[2].start()
    for c in chunks:
        final_xy(c)
    weight_z(0)
    input_gradient(0)
    weight_z(1)
    input_gradient(1)
    for c in chunks:
        final_z(c)
    weight_xy(2)
    weight_end(0)
    weight_end(1)
    for c in chunks:
        gather_xy(c)
    weight_z(2)
    for c in chunks:
        gather_core(c)
    weight_end(2)
    wait(g_core)


def unpack_kernel(gath, wg_ref, dx_in, fin_ref, mod_ref, in_ref, bias_ref, wg_out, dx_hbm, small, sem):
    part = dx_in.shape[0] // sem.shape[0]
    dx_copies = [
        pltpu.make_async_copy(dx_in.at[pl.ds(k * part, part)], dx_hbm.at[pl.ds(k * part, part)], sem.at[k])
        for k in range(sem.shape[0])
    ]
    for c in dx_copies:
        c.start()
    nc, cores, chips, er, cwc = gath.shape
    n_tm = cores * chips
    d_model = fin_ref.shape[1]
    taps_cl, chans = in_ref.shape
    pieces = d_model // chans
    for a, c, k, lo, mid, end in places(n_tm, fin_ref.shape[0] // er, nc, cwc, d_model, chans):
        at = slice(k * er, (k + 1) * er)
        part = gath.at[c, a % cores, a // cores]
        if mid > lo:
            fin_ref[at, lo:mid] = part[:, : mid - lo].astype(F32)
        if end > mid:
            small[at, mid - d_model : end - d_model] = part[:, mid - lo : end - lo].astype(F32)
    in_ref[...] = small[:taps_cl, :]
    bias_ref[...] = small[taps_cl : taps_cl + 1, :]
    for b in range(2):
        for p in range(pieces):
            at = taps_cl + 1 + b * pieces + p
            mod_ref[b : b + 1, p * chans : (p + 1) * chans] = small[at : at + 1, :]
    wg_out[...] = wg_ref[...]
    for c in dx_copies:
        c.wait()


def local(n_tm, n_seq, latents, hidden, grad_out, conv_in_w, conv_in_b, conv_w, final_w, modulation, clip_start):
    slab, cl, width = latents.shape
    taps, chans = conv_w.shape[:2]
    tokens, d_model = hidden.shape
    rows = chans // (n_tm * n_seq)
    block = n_seq * rows
    chips = n_tm // CORES
    w_in = conv_in_w.transpose(0, 2, 1).reshape(taps * cl, chans)
    bias = conv_in_b.reshape(1, chans)
    e = cl * PATCH
    er = 16
    parts = n_tm // (e // er)
    lanes = -(-(d_model + chans) // (parts * 128))
    nc = max(c for c in range(1, CHUNKS + 1) if lanes % c == 0)
    cw = lanes // nc * 128
    vmem = pl.BlockSpec(memory_space=pltpu.VMEM)
    hbm = pl.BlockSpec(memory_space=pltpu.HBM)
    smem = pl.BlockSpec(memory_space=pltpu.SMEM)
    dma = pltpu.SemaphoreType.DMA
    nt, ns = chips - 1, n_seq - 1

    def b16(*shape):
        return pltpu.VMEM(shape, BF16)

    def f32(*shape):
        return pltpu.VMEM(shape, F32)

    def in_hbm(x):
        return pltpu.with_memory_space_constraint(x, pltpu.HBM)

    dx, wg, gath = pl.pallas_call(
        functools.partial(main_kernel, n_tm, n_seq),
        out_shape=(
            b16(tokens, d_model),
            f32(taps, rows, chans),
            b16(nc, CORES, chips, er, cw),
        ),
        in_specs=[hbm] * 9,
        out_specs=(vmem, vmem, vmem),
        scratch_shapes=[
            pltpu.SMEM(clip_start.shape, jnp.int32),
            b16(taps * cl, chans),
            f32(1, chans),
            b16(e, d_model),
            f32(2, d_model),
            b16(slab + HALO, cl, width),
            b16(slab, cl, width),
            f32(slab + 2 - HALO, chans, width),
            b16(slab, chans, width),
            b16(tokens, d_model),
            b16(tokens, d_model),
            f32(tokens, 128),
            b16(chans, 4 * cl),
            b16(slab + 2, 4 * cl, width),
            b16(taps + 3, chans, chans),
            b16(slab + 2, chans, width),
            f32(slab + 2, chans, width),
            b16(slab + 2, chans, width),
            f32(slab + 2, taps * cl, width),
            f32(4 * cl, chans),
            f32(slab + HALO, cl, width),
            b16(HALO, cl, width),
            b16(slab, cl, width),
            b16(n_seq, cl, width),
            b16(n_seq, cl, width),
            b16(taps, CORES, chips, block, chans),
            b16(taps, chips, block, chans),
            b16(taps, chips, block, chans),
            b16(taps, nt, block, chans),
            b16(taps, n_seq, rows, chans),
            b16(taps, ns, rows, chans),
            b16(width, width),
            b16(tokens, e),
            f32(e, d_model),
            f32(8, d_model),
            b16(nc, CORES, chips, er, cw),
            b16(nc, chips, er, cw),
            b16(nc, chips, er, cw),
            b16(nc, nt, er, cw),
            b16(nc, n_seq, er, cw),
            dma((9,)), dma((slab,)), dma(()), dma(()), dma((n_seq,)), dma((n_seq,)), dma((ns,)), dma((ns,)),
            dma((taps,)), dma((taps,)), dma((taps, nt)), dma((taps, nt)), dma((taps, ns)), dma((taps, ns)),
            dma((nc,)), dma((nc,)), dma((nc, nt)), dma((nc, nt)), dma((nc, ns)), dma((nc, ns)),
            dma((nc, nt)), dma((nc, nt)), dma((nc,)), dma((nc,)),
        ],
        compiler_params=pltpu.CompilerParams(
            vmem_limit_bytes=MAIN_VMEM, collective_id=0, has_side_effects=True
        ),
        name="main",
    )(*[in_hbm(x) for x in (clip_start, latents, hidden, grad_out, w_in, bias, conv_w, final_w.T, modulation)])
    fin, mod, w_in_grad, bias_grad, wg, dx = pl.pallas_call(
        unpack_kernel,
        out_shape=(
            jax.ShapeDtypeStruct((e, d_model), F32),
            jax.ShapeDtypeStruct((2, d_model), F32),
            jax.ShapeDtypeStruct((taps * cl, chans), F32),
            jax.ShapeDtypeStruct((1, chans), F32),
            jax.ShapeDtypeStruct((taps, rows, chans), F32),
            jax.ShapeDtypeStruct((tokens, d_model), BF16),
        ),
        in_specs=[vmem, vmem, vmem],
        out_specs=(vmem,) * 5 + (hbm,),
        scratch_shapes=[f32(e, chans), dma((4,))],
        compiler_params=pltpu.CompilerParams(vmem_limit_bytes=SMALL_VMEM),
        name="unpack",
    )(gath, wg, dx)
    return (
        dx,
        wg.transpose(1, 0, 2),
        w_in_grad.reshape(taps, cl, chans).transpose(0, 2, 1),
        bias_grad.reshape(chans),
        fin.T,
        mod,
    )


def solution(mesh):
    return jax.shard_map(
        functools.partial(local, mesh.shape["tm"], mesh.shape["seq"]),
        mesh=mesh,
        in_specs=(
            P("tm", None, "seq"),
            P(("tm", "seq"), None),
            P("tm", None, "seq"),
            P(),
            P(),
            P(),
            P(),
            P(),
            P(),
        ),
        out_specs=(P(("tm", "seq"), None), P(("tm", "seq"), None, None), P(), P(), P(), P()),
        check_vma=False,
    )
```

```python
import functools

import jax
import jax.numpy as jnp
from jax import lax
from jax.experimental import pallas as pl
from jax.experimental.pallas import tpu as pltpu
from jax.sharding import PartitionSpec as P

F32 = jnp.float32
BF16 = jnp.bfloat16
MESH = pl.DeviceIdType.MESH
PATCH = 4
CORES = 2
TAPS = 3
HALO = 4
CHUNKS = 2
MAIN_VMEM = 46 * 1024 * 1024
SMALL_VMEM = 12 * 1024 * 1024


def dot(a, b, ca, cb):
    return lax.dot_general(a, b, (((ca,), (cb,)), ((), ())), preferred_element_type=F32)


def load_in_weights(w_in_ref, b_ref, w64):
    bias = b_ref[...]
    hi = bias.astype(BF16)
    mid = (bias - hi.astype(F32)).astype(BF16)
    lo = (bias - hi.astype(F32) - mid.astype(F32)).astype(BF16)
    pad = jnp.zeros((16 - 3, bias.shape[1]), F32)
    rows = jnp.concatenate(
        [w_in_ref[...].astype(F32), hi.astype(F32), mid.astype(F32), lo.astype(F32), pad], axis=0
    )
    w64[...] = rows.T.astype(BF16)


def places(n_tm, groups, nc, width, wide, narrow):
    parts = n_tm // groups
    for a in range(n_tm):
        for c in range(nc):
            lo = ((a % parts) * nc + c) * width
            mid = min(max(lo, wide), lo + width)
            end = min(max(lo, wide + narrow), lo + width)
            yield a, c, a // parts, lo, mid, end


def sigmoid(x):
    return 0.5 * jnp.tanh(0.5 * x) + 0.5


def main_kernel(
    n_tm, n_seq,
    clip_hbm, lat_hbm, hid_hbm, grad_hbm, w_in_hbm, b_hbm, w_hbm, fw_hbm, modu_hbm,
    dx_ref, wg_ref, gath,
    clip_ref, w_in_ref, b_ref, fw_ref, modu_ref,
    latx, lat_own, slope, g, hid, nb, inv, w64, z, tab, act, ga, gp, parts, misc, lg, lgh, lgs, tok, tokh,
    w4, wcore, whalf, wrecv, wsum, wrecv2,
    spread, tgs, facc, macc, f4, fcore, fhalf, frecv, fall,
    s_in, s_g_in, s_lat, r_lat, s_halo, r_halo, s_tok, r_tok,
    s_wc, r_wc, s_w, r_w, s_w2, r_w2,
    s_fc, r_fc, s_f, r_f, s_f2, r_f2, s_g, r_g, s_gc, r_gc,
):
    i = lax.axis_index("tm")
    j = lax.axis_index("seq")
    chips = n_tm // CORES
    core = lax.rem(i, CORES)
    chip = lax.div(i, CORES)
    other = CORES - 1 - core
    sibling = (chip * CORES + other, j)
    tms = [(d, lax.rem(chip + d, chips)) for d in range(1, chips)]
    seqs = [(d, lax.rem(j + d, n_seq)) for d in range(1, n_seq)]
    slab, chans = g.shape[:2]
    cl, width = latx.shape[1:]
    frames = clip_ref.shape[0]
    d_model = hid.shape[1]
    first = i * slab

    loads = [
        pltpu.make_async_copy(src, dst, s_in.at[k])
        for k, (src, dst) in enumerate(
            [
                (clip_hbm, clip_ref),
                (w_hbm, tab.at[pl.ds(0, TAPS)]),
                (w_in_hbm, w_in_ref),
                (b_hbm, b_ref),
                (lat_hbm, latx.at[pl.ds(HALO, slab)]),
                (hid_hbm, hid),
                (fw_hbm, fw_ref),
                (modu_hbm, modu_ref),
                (lat_hbm, lat_own),
            ]
        )
    ]
    own_clip, own_w, own_w_in, own_b, own_lat, own_hid, own_fw, own_modu, own_lat2 = loads
    own_g = [pltpu.make_async_copy(grad_hbm.at[t], g.at[t], s_g_in.at[t]) for t in range(slab)]
    for c in [own_w_in, own_b, own_lat2, own_clip, own_w] + own_g + [own_lat, own_fw, own_modu, own_hid]:
        c.start()

    barrier = pltpu.get_barrier_semaphore()
    greeted = [(p * CORES + core, j) for _, p in tms] + [sibling] + [(i, p) for _, p in seqs]
    greeted += [(lax.rem(i + 1, n_tm), p) for p in range(n_seq)] + [(lax.rem(i + n_tm - 1, n_tm), j)]
    for to in greeted:
        pl.semaphore_signal(barrier, inc=1, device_id=to, device_id_type=MESH)

    def copy(src, dst, send, recv, to):
        return pltpu.make_async_remote_copy(
            src_ref=src, dst_ref=dst, send_sem=send, recv_sem=recv, device_id=to, device_id_type=MESH
        )

    def lat_copy(to):
        return copy(lat_hbm.at[pl.ds(slab - HALO, HALO)], latx.at[pl.ds(0, HALO)], s_lat, r_lat, (to, j))

    def clip_of(frame):
        return clip_ref[jnp.clip(frame, 0, frames - 1)]

    def source(frame, tap):
        return jnp.maximum(frame - tap, clip_of(frame))

    n = width // PATCH
    e = cl * PATCH
    row = lax.broadcasted_iota(jnp.int32, (width, width), 0)
    col = lax.broadcasted_iota(jnp.int32, (width, width), 1)
    spread[...] = jnp.where(row == lax.rem(col, n) * PATCH + lax.div(col, n), 1.0, 0.0).astype(BF16)
    row = lax.broadcasted_iota(jnp.int32, (e, e), 0)
    col = lax.broadcasted_iota(jnp.int32, (e, e), 1)
    order = jnp.where(row == lax.rem(col, cl) * PATCH + lax.div(col, cl), 1.0, 0.0).astype(BF16)
    def prepare(r, held, base):
        frame = first + r - 2
        for tap in range(TAPS):
            row = jnp.clip(source(frame, tap) - base, 0, held.shape[0] - 1)
            z[r, tap * cl : (tap + 1) * cl] = held[row]
        z[r, TAPS * cl :] = jnp.ones((cl, width), BF16)
        pre = dot(w64[...], z[r], 1, 0)
        sig = sigmoid(pre)
        a = pre * sig
        act[r] = a.astype(BF16)
        return sig + a * (1.0 - sig)

    own_w_in.wait()
    own_b.wait()
    load_in_weights(w_in_ref, b_ref, w64)
    own_clip.wait()
    own_lat2.wait()
    for r in range(HALO, slab + 2):
        slope[r - HALO] = prepare(r, lat_own, first)
    own_w.wait()
    later = tab[1].astype(F32) + tab[2].astype(F32)
    tab[TAPS] = later.astype(BF16)
    tab[TAPS + 1] = (later + tab[0].astype(F32)).astype(BF16)
    tab[TAPS + 2] = jnp.zeros_like(tab[TAPS + 2])

    def choice(t, back):
        start = clip_of(first + t)
        back1 = start < first + t
        back2 = start < first + t - 1
        if back == 0:
            return jnp.where(back1, 0, TAPS + 1)
        if back == 1:
            return jnp.where(back2, 1, jnp.where(back1, TAPS, TAPS + 2))
        return jnp.where(back2, 2, TAPS + 2)

    def grad_act(r):
        ga[r] = sum(
            dot(tab[choice(r - 2 + back, back)], g[r - 2 + back], 0, 0)
            for back in range(TAPS)
            if 0 <= r - 2 + back < slab
        )

    own_g[0].wait()
    grad_act(0)
    own_g[1].wait()
    grad_act(1)
    pl.semaphore_wait(barrier, len(greeted))

    @pl.when(i < n_tm - 1)
    def _():
        lat_copy(i + 1).start()

    @pl.when(i == 0)
    def _():
        latx[0:HALO] = jnp.zeros_like(latx[0:HALO])

    for r in range(2, slab + 2):
        if r < slab:
            own_g[r].wait()
        grad_act(r)

    own_lat.wait()

    @pl.when(i < n_tm - 1)
    def _():
        lat_copy(i + 1).wait_send()

    @pl.when(i > 0)
    def _():
        lat_copy(i).wait_recv()

    def finish(r):
        factor = prepare(r, latx, first - HALO) if r < HALO else slope[r - HALO]
        grad_pre = (ga[r] * factor).astype(BF16)
        gp[r] = grad_pre
        parts[r] = dot(w_in_ref[...], grad_pre, 1, 0)

    def scatter(r):
        start = clip_of(first + r - 2)
        back1 = jnp.where(start < first + r - 2, 1.0, 0.0).astype(F32)
        back2 = jnp.where(start < first + r - 3, 1.0, 0.0).astype(F32)
        p0, p1, p2 = [parts[r, tap * cl : (tap + 1) * cl] for tap in range(TAPS)]
        lg[r + 2] += p0 + (1.0 - back1) * (p1 + p2)
        lg[r + 1] += back1 * p1 + (back1 - back2) * p2
        lg[r] += back2 * p2

    lg[...] = jnp.zeros_like(lg)
    for r in range(HALO):
        finish(r)
    for r in range(HALO):
        scatter(r)
    lgh[...] = lg[0:HALO].astype(BF16)

    def halo_copy(to, p):
        return copy(lgh.at[p], tokh.at[j], s_halo.at[p], r_halo.at[j], (to, p))

    @pl.when(i > 0)
    def _():
        for p in range(n_seq):
            halo_copy(i - 1, p).start()

    @pl.when(i == n_tm - 1)
    def _():
        tokh[...] = jnp.zeros_like(tokh)

    for r in range(HALO, slab + 2):
        finish(r)
    for r in range(HALO, slab + 2):
        scatter(r)
    lgs[...] = lg[HALO : HALO + slab].astype(BF16)
    tok_copies = [copy(lgs.at[p], tok.at[j], s_tok.at[d - 1], r_tok.at[d - 1], (i, p)) for d, p in seqs]
    for c in tok_copies:
        c.start()

    rows = chans // (n_tm * n_seq)
    block = n_seq * rows

    def weight(tap):
        total = sum(
            dot(g[t], act[jnp.clip(source(first + t, tap) - first + 2, 0, slab + 1)], 1, 1) for t in range(slab)
        )
        for q in range(chips):
            for c in range(CORES):
                at = (q * CORES + c) * block
                w4[tap, c, q] = total[at : at + block].astype(BF16)

    w_core = [
        copy(w4.at[tap, other], wcore.at[tap], s_wc.at[tap], r_wc.at[tap], sibling) for tap in range(TAPS)
    ]
    w_xy = [
        [
            copy(whalf.at[tap, p], wrecv.at[tap, d - 1], s_w.at[tap, d - 1], r_w.at[tap, d - 1], (p * CORES + core, j))
            for d, p in tms
        ]
        for tap in range(TAPS)
    ]
    w_z = [
        [
            copy(wsum.at[tap, p], wrecv2.at[tap, d - 1], s_w2.at[tap, d - 1], r_w2.at[tap, d - 1], (i, p))
            for d, p in seqs
        ]
        for tap in range(TAPS)
    ]

    def weight_xy(tap):
        w_core[tap].wait()
        whalf[tap] = (w4[tap, core].astype(F32) + wcore[tap].astype(F32)).astype(BF16)
        for c in w_xy[tap]:
            c.start()

    def weight_z(tap):
        for c in w_xy[tap]:
            c.wait()
        total = whalf[tap, chip].astype(F32)
        for k in range(chips - 1):
            total = total + wrecv[tap, k].astype(F32)
        for p in range(n_seq):
            wsum[tap, p] = total[p * rows : (p + 1) * rows].astype(BF16)
        for c in w_z[tap]:
            c.start()

    def weight_end(tap):
        for c in w_z[tap]:
            c.wait()
        total = wsum[tap, j].astype(F32)
        for k in range(n_seq - 1):
            total = total + wrecv2[tap, k].astype(F32)
        wg_ref[tap] = total

    weight(0)
    w_core[0].start()
    weight(1)
    w_core[1].start()
    weight_xy(0)
    own_hid.wait()
    step_rows = 128

    @pl.loop(0, hid.shape[0] // step_rows)
    def _(r):
        at = pl.ds(pl.multiple_of(r * step_rows, step_rows), step_rows)
        h = hid[at, :].astype(F32)
        center = h - jnp.mean(h, axis=1, keepdims=True)
        scaled = lax.rsqrt(jnp.mean(center * center, axis=1, keepdims=True) + 1e-06)
        nb[at, :] = (center * scaled).astype(BF16)
        inv[at, :] = jnp.broadcast_to(scaled, (step_rows, inv.shape[1]))

    weight_xy(1)
    misc[...] = sum(dot(z[r], gp[r], 1, 1) for r in range(slab + 2))

    own_fw.wait()
    own_modu.wait()
    shift = modu_ref[0:1, :]
    scale = 1.0 + modu_ref[1:2, :]

    @pl.when(i > 0)
    def _():
        for p in range(n_seq):
            halo_copy(i - 1, p).wait_send()

    @pl.when(i < n_tm - 1)
    def _():
        for p in range(n_seq):
            copy(lgh.at[0], tokh.at[p], s_halo.at[0], r_halo.at[p], (i, j)).wait_recv()

    for c in tok_copies:
        c.wait()
    tok[j] = lgs[j]

    lat = jnp.concatenate([(tok[r].astype(F32) + tokh[r].astype(F32)).astype(BF16) for r in range(n_seq)], axis=0)
    split = dot(lat, spread[...], 1, 0)
    stack = jnp.concatenate(
        [
            jnp.concatenate([split[r * cl : (r + 1) * cl, q * n : (q + 1) * n] for r in range(n_seq)], axis=1)
            for q in range(PATCH)
        ],
        axis=0,
    )
    tg_t = dot(order, stack.astype(BF16), 1, 0)
    facc[...] = dot(tg_t.astype(BF16), nb[...], 1, 0)
    column = jnp.sum(tg_t, axis=1, keepdims=True)
    tgs[...] = tg_t.T.astype(BF16)

    fw = fw_ref[...].astype(F32)
    macc[0:1] = jnp.sum(fw * column, axis=0, keepdims=True)
    macc[1:2] = jnp.sum(fw * facc[...], axis=0, keepdims=True)
    facc[...] = facc[...] * scale + column * shift

    pieces = d_model // chans
    small = jnp.concatenate(
        [misc[0 : TAPS * cl + 1, :]]
        + [macc[b : b + 1, p * chans : (p + 1) * chans] for b in range(2) for p in range(pieces)]
        + [jnp.zeros((e - TAPS * cl - 1 - 2 * pieces, chans), F32)],
        axis=0,
    )
    nc, er, cwc = f4.shape[0], f4.shape[3], f4.shape[4]
    for a, c, k, lo, mid, end in places(n_tm, e // er, nc, cwc, d_model, chans):
        at = slice(k * er, (k + 1) * er)
        to = f4.at[c, a % CORES, a // CORES]
        if mid > lo:
            to[:, : mid - lo] = facc[at, lo:mid].astype(BF16)
        if end > mid:
            to[:, mid - lo : end - lo] = small[at, mid - d_model : end - d_model].astype(BF16)
        if lo + cwc > end:
            to[:, end - lo :] = jnp.zeros((er, lo + cwc - end), BF16)
    chunks = range(nc)
    f_core = [copy(f4.at[c, other], fcore.at[c], s_fc.at[c], r_fc.at[c], sibling) for c in chunks]
    for c in chunks:
        f_core[c].start()

    half = hid.shape[0] // 2

    def input_gradient(k):
        at = slice(k * half, (k + 1) * half)
        normed = nb[at, :].astype(F32)
        ng = dot(tgs[at, :], fw_ref[...], 1, 0) * scale
        m1 = jnp.mean(ng, axis=1, keepdims=True)
        m2 = jnp.mean(ng * normed, axis=1, keepdims=True)
        dx_ref[at, :] = (inv[at, 0:1] * (ng - m1 - normed * m2)).astype(BF16)

    f_xy = [
        [
            copy(fhalf.at[c, p], frecv.at[c, d - 1], s_f.at[c, d - 1], r_f.at[c, d - 1], (p * CORES + core, j))
            for d, p in tms
        ]
        for c in chunks
    ]
    f_z = [
        [copy(fall.at[c, j], fall.at[c, j], s_f2.at[c, d - 1], r_f2.at[c, d - 1], (i, p)) for d, p in seqs]
        for c in chunks
    ]
    g_xy = [
        [
            copy(
                gath.at[c, core, chip], gath.at[c, core, chip], s_g.at[c, d - 1], r_g.at[c, d - 1],
                (p * CORES + core, j),
            )
            for d, p in tms
        ]
        for c in chunks
    ]
    g_core = [copy(gath.at[c, core], gath.at[c, core], s_gc.at[c], r_gc.at[c], sibling) for c in chunks]

    def start(copies):
        for c in copies:
            c.start()

    def wait(copies):
        for c in copies:
            c.wait()

    def final_xy(c):
        f_core[c].wait()
        for q in range(chips):
            fhalf[c, q] = (f4[c, core, q].astype(F32) + fcore[c, q].astype(F32)).astype(BF16)
        start(f_xy[c])

    def final_z(c):
        wait(f_xy[c])
        total = fhalf[c, chip].astype(F32)
        for k in range(chips - 1):
            total = total + frecv[c, k].astype(F32)
        fall[c, j] = total.astype(BF16)
        start(f_z[c])

    def gather_xy(c):
        wait(f_z[c])
        total = fall[c, 0].astype(F32)
        for k in range(1, n_seq):
            total = total + fall[c, k].astype(F32)
        gath[c, core, chip] = total.astype(BF16)
        start(g_xy[c])

    def gather_core(c):
        wait(g_xy[c])
        g_core[c].start()

    weight(2)
    w_core[2].start()
    for c in chunks:
        final_xy(c)
    weight_z(0)
    input_gradient(0)
    input_gradient(1)
    for c in chunks:
        final_z(c)
    weight_xy(2)
    weight_end(0)
    for c in chunks:
        gather_xy(c)
    weight_z(1)
    weight_z(2)
    for c in chunks:
        gather_core(c)
    weight_end(1)
    weight_end(2)
    wait(g_core)


def unpack_kernel(gath, wg_ref, dx_in, fin_ref, mod_ref, in_ref, bias_ref, wg_out, dx_hbm, small, sem):
    part = dx_in.shape[0] // sem.shape[0]
    dx_copies = [
        pltpu.make_async_copy(dx_in.at[pl.ds(k * part, part)], dx_hbm.at[pl.ds(k * part, part)], sem.at[k])
        for k in range(sem.shape[0])
    ]
    for c in dx_copies:
        c.start()
    nc, cores, chips, er, cwc = gath.shape
    n_tm = cores * chips
    d_model = fin_ref.shape[1]
    taps_cl, chans = in_ref.shape
    pieces = d_model // chans
    for a, c, k, lo, mid, end in places(n_tm, fin_ref.shape[0] // er, nc, cwc, d_model, chans):
        at = slice(k * er, (k + 1) * er)
        part = gath.at[c, a % cores, a // cores]
        if mid > lo:
            fin_ref[at, lo:mid] = part[:, : mid - lo].astype(F32)
        if end > mid:
            small[at, mid - d_model : end - d_model] = part[:, mid - lo : end - lo].astype(F32)
    in_ref[...] = small[:taps_cl, :]
    bias_ref[...] = small[taps_cl : taps_cl + 1, :]
    for b in range(2):
        for p in range(pieces):
            at = taps_cl + 1 + b * pieces + p
            mod_ref[b : b + 1, p * chans : (p + 1) * chans] = small[at : at + 1, :]
    wg_out[...] = wg_ref[...]
    for c in dx_copies:
        c.wait()


def local(n_tm, n_seq, latents, hidden, grad_out, conv_in_w, conv_in_b, conv_w, final_w, modulation, clip_start):
    slab, cl, width = latents.shape
    taps, chans = conv_w.shape[:2]
    tokens, d_model = hidden.shape
    rows = chans // (n_tm * n_seq)
    block = n_seq * rows
    chips = n_tm // CORES
    w_in = conv_in_w.transpose(0, 2, 1).reshape(taps * cl, chans)
    bias = conv_in_b.reshape(1, chans)
    e = cl * PATCH
    er = 16
    parts = n_tm // (e // er)
    lanes = -(-(d_model + chans) // (parts * 128))
    nc = max(c for c in range(1, CHUNKS + 1) if lanes % c == 0)
    cw = lanes // nc * 128
    vmem = pl.BlockSpec(memory_space=pltpu.VMEM)
    hbm = pl.BlockSpec(memory_space=pltpu.HBM)
    smem = pl.BlockSpec(memory_space=pltpu.SMEM)
    dma = pltpu.SemaphoreType.DMA
    nt, ns = chips - 1, n_seq - 1

    def b16(*shape):
        return pltpu.VMEM(shape, BF16)

    def f32(*shape):
        return pltpu.VMEM(shape, F32)

    def in_hbm(x):
        return pltpu.with_memory_space_constraint(x, pltpu.HBM)

    dx, wg, gath = pl.pallas_call(
        functools.partial(main_kernel, n_tm, n_seq),
        out_shape=(
            b16(tokens, d_model),
            f32(taps, rows, chans),
            b16(nc, CORES, chips, er, cw),
        ),
        in_specs=[hbm] * 9,
        out_specs=(vmem, vmem, vmem),
        scratch_shapes=[
            pltpu.SMEM(clip_start.shape, jnp.int32),
            b16(taps * cl, chans),
            f32(1, chans),
            b16(e, d_model),
            f32(2, d_model),
            b16(slab + HALO, cl, width),
            b16(slab, cl, width),
            f32(slab + 2 - HALO, chans, width),
            b16(slab, chans, width),
            b16(tokens, d_model),
            b16(tokens, d_model),
            f32(tokens, 128),
            b16(chans, 4 * cl),
            b16(slab + 2, 4 * cl, width),
            b16(taps + 3, chans, chans),
            b16(slab + 2, chans, width),
            f32(slab + 2, chans, width),
            b16(slab + 2, chans, width),
            f32(slab + 2, taps * cl, width),
            f32(4 * cl, chans),
            f32(slab + HALO, cl, width),
            b16(HALO, cl, width),
            b16(slab, cl, width),
            b16(n_seq, cl, width),
            b16(n_seq, cl, width),
            b16(taps, CORES, chips, block, chans),
            b16(taps, chips, block, chans),
            b16(taps, chips, block, chans),
            b16(taps, nt, block, chans),
            b16(taps, n_seq, rows, chans),
            b16(taps, ns, rows, chans),
            b16(width, width),
            b16(tokens, e),
            f32(e, d_model),
            f32(8, d_model),
            b16(nc, CORES, chips, er, cw),
            b16(nc, chips, er, cw),
            b16(nc, chips, er, cw),
            b16(nc, nt, er, cw),
            b16(nc, n_seq, er, cw),
            dma((9,)), dma((slab,)), dma(()), dma(()), dma((n_seq,)), dma((n_seq,)), dma((ns,)), dma((ns,)),
            dma((taps,)), dma((taps,)), dma((taps, nt)), dma((taps, nt)), dma((taps, ns)), dma((taps, ns)),
            dma((nc,)), dma((nc,)), dma((nc, nt)), dma((nc, nt)), dma((nc, ns)), dma((nc, ns)),
            dma((nc, nt)), dma((nc, nt)), dma((nc,)), dma((nc,)),
        ],
        compiler_params=pltpu.CompilerParams(
            vmem_limit_bytes=MAIN_VMEM, collective_id=0, has_side_effects=True
        ),
        name="main",
    )(*[in_hbm(x) for x in (clip_start, latents, hidden, grad_out, w_in, bias, conv_w, final_w.T, modulation)])
    fin, mod, w_in_grad, bias_grad, wg, dx = pl.pallas_call(
        unpack_kernel,
        out_shape=(
            jax.ShapeDtypeStruct((e, d_model), F32),
            jax.ShapeDtypeStruct((2, d_model), F32),
            jax.ShapeDtypeStruct((taps * cl, chans), F32),
            jax.ShapeDtypeStruct((1, chans), F32),
            jax.ShapeDtypeStruct((taps, rows, chans), F32),
            jax.ShapeDtypeStruct((tokens, d_model), BF16),
        ),
        in_specs=[vmem, vmem, vmem],
        out_specs=(vmem,) * 5 + (hbm,),
        scratch_shapes=[f32(e, chans), dma((4,))],
        compiler_params=pltpu.CompilerParams(vmem_limit_bytes=SMALL_VMEM),
        name="unpack",
    )(gath, wg, dx)
    return (
        dx,
        wg.transpose(1, 0, 2),
        w_in_grad.reshape(taps, cl, chans).transpose(0, 2, 1),
        bias_grad.reshape(chans),
        fin.T,
        mod,
    )


def solution(mesh):
    return jax.shard_map(
        functools.partial(local, mesh.shape["tm"], mesh.shape["seq"]),
        mesh=mesh,
        in_specs=(
            P("tm", None, "seq"),
            P(("tm", "seq"), None),
            P("tm", None, "seq"),
            P(),
            P(),
            P(),
            P(),
            P(),
            P(),
        ),
        out_specs=(P(("tm", "seq"), None), P(("tm", "seq"), None, None), P(), P(), P(), P()),
        check_vma=False,
    )
```

```python
import functools

import jax
import jax.numpy as jnp
from jax import lax
from jax.experimental import pallas as pl
from jax.experimental.pallas import tpu as pltpu
from jax.sharding import PartitionSpec as P

F32 = jnp.float32
BF16 = jnp.bfloat16
MESH = pl.DeviceIdType.MESH
PATCH = 4
CORES = 2
TAPS = 3
HALO = 4
CHUNKS = 2
MAIN_VMEM = 46 * 1024 * 1024
SMALL_VMEM = 12 * 1024 * 1024


def dot(a, b, ca, cb):
    return lax.dot_general(a, b, (((ca,), (cb,)), ((), ())), preferred_element_type=F32)


def load_in_weights(w_in_ref, b_ref, w64):
    bias = b_ref[...]
    hi = bias.astype(BF16)
    mid = (bias - hi.astype(F32)).astype(BF16)
    lo = (bias - hi.astype(F32) - mid.astype(F32)).astype(BF16)
    pad = jnp.zeros((16 - 3, bias.shape[1]), F32)
    rows = jnp.concatenate(
        [w_in_ref[...].astype(F32), hi.astype(F32), mid.astype(F32), lo.astype(F32), pad], axis=0
    )
    w64[...] = rows.T.astype(BF16)


def places(n_tm, groups, nc, width, wide, narrow):
    parts = n_tm // groups
    for a in range(n_tm):
        for c in range(nc):
            lo = ((a % parts) * nc + c) * width
            mid = min(max(lo, wide), lo + width)
            end = min(max(lo, wide + narrow), lo + width)
            yield a, c, a // parts, lo, mid, end


def sigmoid(x):
    return 0.5 * jnp.tanh(0.5 * x) + 0.5


def main_kernel(
    n_tm, n_seq,
    clip_hbm, lat_hbm, hid_hbm, grad_hbm, w_in_hbm, b_hbm, w_hbm, fw_hbm, modu_hbm,
    dx_ref, wg_ref, gath,
    clip_ref, w_in_ref, b_ref, fw_ref, modu_ref,
    latx, lat_own, slope, g, hid, nb, inv, w64, z, tab, act, ga, gp, parts, misc, lg, lgh, lgs, tok, tokh,
    w4, wcore, whalf, wrecv, wsum, wrecv2,
    spread, tgs, facc, macc, f4, fcore, fhalf, frecv, fall,
    s_in, s_g_in, s_lat, r_lat, s_halo, r_halo, s_tok, r_tok,
    s_wc, r_wc, s_w, r_w, s_w2, r_w2,
    s_fc, r_fc, s_f, r_f, s_f2, r_f2, s_g, r_g, s_gc, r_gc,
):
    i = lax.axis_index("tm")
    j = lax.axis_index("seq")
    chips = n_tm // CORES
    core = lax.rem(i, CORES)
    chip = lax.div(i, CORES)
    other = CORES - 1 - core
    sibling = (chip * CORES + other, j)
    tms = [(d, lax.rem(chip + d, chips)) for d in range(1, chips)]
    seqs = [(d, lax.rem(j + d, n_seq)) for d in range(1, n_seq)]
    slab, chans = g.shape[:2]
    cl, width = latx.shape[1:]
    frames = clip_ref.shape[0]
    d_model = hid.shape[1]
    first = i * slab

    loads = [
        pltpu.make_async_copy(src, dst, s_in.at[k])
        for k, (src, dst) in enumerate(
            [
                (clip_hbm, clip_ref),
                (w_hbm, tab.at[pl.ds(0, TAPS)]),
                (w_in_hbm, w_in_ref),
                (b_hbm, b_ref),
                (lat_hbm, latx.at[pl.ds(HALO, slab)]),
                (hid_hbm, hid),
                (fw_hbm, fw_ref),
                (modu_hbm, modu_ref),
                (lat_hbm, lat_own),
            ]
        )
    ]
    own_clip, own_w, own_w_in, own_b, own_lat, own_hid, own_fw, own_modu, own_lat2 = loads
    own_g = [pltpu.make_async_copy(grad_hbm.at[t], g.at[t], s_g_in.at[t]) for t in range(slab)]
    for c in [own_w_in, own_b, own_lat2, own_clip, own_w] + own_g + [own_lat, own_fw, own_modu, own_hid]:
        c.start()

    barrier = pltpu.get_barrier_semaphore()
    greeted = [(p * CORES + core, j) for _, p in tms] + [sibling] + [(i, p) for _, p in seqs]
    greeted += [(lax.rem(i + 1, n_tm), p) for p in range(n_seq)] + [(lax.rem(i + n_tm - 1, n_tm), j)]
    for to in greeted:
        pl.semaphore_signal(barrier, inc=1, device_id=to, device_id_type=MESH)

    def copy(src, dst, send, recv, to):
        return pltpu.make_async_remote_copy(
            src_ref=src, dst_ref=dst, send_sem=send, recv_sem=recv, device_id=to, device_id_type=MESH
        )

    def lat_copy(to):
        return copy(lat_hbm.at[pl.ds(slab - HALO, HALO)], latx.at[pl.ds(0, HALO)], s_lat, r_lat, (to, j))

    def clip_of(frame):
        return clip_ref[jnp.clip(frame, 0, frames - 1)]

    def source(frame, tap):
        return jnp.maximum(frame - tap, clip_of(frame))

    n = width // PATCH
    e = cl * PATCH
    row = lax.broadcasted_iota(jnp.int32, (width, width), 0)
    col = lax.broadcasted_iota(jnp.int32, (width, width), 1)
    spread[...] = jnp.where(row == lax.rem(col, n) * PATCH + lax.div(col, n), 1.0, 0.0).astype(BF16)
    row = lax.broadcasted_iota(jnp.int32, (e, e), 0)
    col = lax.broadcasted_iota(jnp.int32, (e, e), 1)
    order = jnp.where(row == lax.rem(col, cl) * PATCH + lax.div(col, cl), 1.0, 0.0).astype(BF16)
    def prepare(r, held, base):
        frame = first + r - 2
        for tap in range(TAPS):
            row = jnp.clip(source(frame, tap) - base, 0, held.shape[0] - 1)
            z[r, tap * cl : (tap + 1) * cl] = held[row]
        z[r, TAPS * cl :] = jnp.ones((cl, width), BF16)
        pre = dot(w64[...], z[r], 1, 0)
        sig = sigmoid(pre)
        a = pre * sig
        act[r] = a.astype(BF16)
        return sig + a * (1.0 - sig)

    own_w_in.wait()
    own_b.wait()
    load_in_weights(w_in_ref, b_ref, w64)
    own_clip.wait()
    own_lat2.wait()
    for r in range(HALO, slab + 2):
        slope[r - HALO] = prepare(r, lat_own, first)
    own_w.wait()
    later = tab[1].astype(F32) + tab[2].astype(F32)
    tab[TAPS] = later.astype(BF16)
    tab[TAPS + 1] = (later + tab[0].astype(F32)).astype(BF16)
    tab[TAPS + 2] = jnp.zeros_like(tab[TAPS + 2])

    def choice(t, back):
        start = clip_of(first + t)
        back1 = start < first + t
        back2 = start < first + t - 1
        if back == 0:
            return jnp.where(back1, 0, TAPS + 1)
        if back == 1:
            return jnp.where(back2, 1, jnp.where(back1, TAPS, TAPS + 2))
        return jnp.where(back2, 2, TAPS + 2)

    def grad_act(r):
        ga[r] = sum(
            dot(tab[choice(r - 2 + back, back)], g[r - 2 + back], 0, 0)
            for back in range(TAPS)
            if 0 <= r - 2 + back < slab
        )

    own_g[0].wait()
    grad_act(0)
    own_g[1].wait()
    grad_act(1)
    pl.semaphore_wait(barrier, len(greeted))

    @pl.when(i < n_tm - 1)
    def _():
        lat_copy(i + 1).start()

    @pl.when(i == 0)
    def _():
        latx[0:HALO] = jnp.zeros_like(latx[0:HALO])

    for r in range(2, slab + 2):
        if r < slab:
            own_g[r].wait()
        grad_act(r)

    own_lat.wait()

    @pl.when(i < n_tm - 1)
    def _():
        lat_copy(i + 1).wait_send()

    @pl.when(i > 0)
    def _():
        lat_copy(i).wait_recv()

    def finish(r):
        factor = prepare(r, latx, first - HALO) if r < HALO else slope[r - HALO]
        grad_pre = (ga[r] * factor).astype(BF16)
        gp[r] = grad_pre
        parts[r] = dot(w_in_ref[...], grad_pre, 1, 0)

    def scatter(r):
        start = clip_of(first + r - 2)
        back1 = jnp.where(start < first + r - 2, 1.0, 0.0).astype(F32)
        back2 = jnp.where(start < first + r - 3, 1.0, 0.0).astype(F32)
        p0, p1, p2 = [parts[r, tap * cl : (tap + 1) * cl] for tap in range(TAPS)]
        lg[r + 2] += p0 + (1.0 - back1) * (p1 + p2)
        lg[r + 1] += back1 * p1 + (back1 - back2) * p2
        lg[r] += back2 * p2

    lg[...] = jnp.zeros_like(lg)
    for r in range(HALO):
        finish(r)
    for r in range(HALO):
        scatter(r)
    lgh[...] = lg[0:HALO].astype(BF16)

    def halo_copy(to, p):
        return copy(lgh.at[p], tokh.at[j], s_halo.at[p], r_halo.at[j], (to, p))

    @pl.when(i > 0)
    def _():
        for p in range(n_seq):
            halo_copy(i - 1, p).start()

    @pl.when(i == n_tm - 1)
    def _():
        tokh[...] = jnp.zeros_like(tokh)

    for r in range(HALO, slab + 2):
        finish(r)
    for r in range(HALO, slab + 2):
        scatter(r)
    lgs[...] = lg[HALO : HALO + slab].astype(BF16)
    tok_copies = [copy(lgs.at[p], tok.at[j], s_tok.at[d - 1], r_tok.at[d - 1], (i, p)) for d, p in seqs]
    for c in tok_copies:
        c.start()

    rows = chans // (n_tm * n_seq)
    block = n_seq * rows

    def weight(tap):
        total = sum(
            dot(g[t], act[jnp.clip(source(first + t, tap) - first + 2, 0, slab + 1)], 1, 1) for t in range(slab)
        )
        for q in range(chips):
            for c in range(CORES):
                at = (q * CORES + c) * block
                w4[tap, c, q] = total[at : at + block].astype(BF16)

    w_core = [
        copy(w4.at[tap, other], wcore.at[tap], s_wc.at[tap], r_wc.at[tap], sibling) for tap in range(TAPS)
    ]
    w_xy = [
        [
            copy(whalf.at[tap, p], wrecv.at[tap, d - 1], s_w.at[tap, d - 1], r_w.at[tap, d - 1], (p * CORES + core, j))
            for d, p in tms
        ]
        for tap in range(TAPS)
    ]
    w_z = [
        [
            copy(wsum.at[tap, p], wrecv2.at[tap, d - 1], s_w2.at[tap, d - 1], r_w2.at[tap, d - 1], (i, p))
            for d, p in seqs
        ]
        for tap in range(TAPS)
    ]

    def weight_xy(tap):
        w_core[tap].wait()
        whalf[tap] = (w4[tap, core].astype(F32) + wcore[tap].astype(F32)).astype(BF16)
        for c in w_xy[tap]:
            c.start()

    def weight_z(tap):
        for c in w_xy[tap]:
            c.wait()
        total = whalf[tap, chip].astype(F32)
        for k in range(chips - 1):
            total = total + wrecv[tap, k].astype(F32)
        for p in range(n_seq):
            wsum[tap, p] = total[p * rows : (p + 1) * rows].astype(BF16)
        for c in w_z[tap]:
            c.start()

    def weight_end(tap):
        for c in w_z[tap]:
            c.wait()
        total = wsum[tap, j].astype(F32)
        for k in range(n_seq - 1):
            total = total + wrecv2[tap, k].astype(F32)
        wg_ref[tap] = total

    weight(0)
    w_core[0].start()
    weight(1)
    w_core[1].start()
    weight_xy(0)
    own_hid.wait()
    step_rows = 128

    @pl.loop(0, hid.shape[0] // step_rows)
    def _(r):
        at = pl.ds(pl.multiple_of(r * step_rows, step_rows), step_rows)
        h = hid[at, :].astype(F32)
        center = h - jnp.mean(h, axis=1, keepdims=True)
        scaled = lax.rsqrt(jnp.mean(center * center, axis=1, keepdims=True) + 1e-06)
        nb[at, :] = (center * scaled).astype(BF16)
        inv[at, :] = jnp.broadcast_to(scaled, (step_rows, inv.shape[1]))

    weight_xy(1)
    misc[...] = sum(dot(z[r], gp[r], 1, 1) for r in range(slab + 2))

    own_fw.wait()
    own_modu.wait()
    shift = modu_ref[0:1, :]
    scale = 1.0 + modu_ref[1:2, :]

    @pl.when(i > 0)
    def _():
        for p in range(n_seq):
            halo_copy(i - 1, p).wait_send()

    @pl.when(i < n_tm - 1)
    def _():
        for p in range(n_seq):
            copy(lgh.at[0], tokh.at[p], s_halo.at[0], r_halo.at[p], (i, j)).wait_recv()

    for c in tok_copies:
        c.wait()
    tok[j] = lgs[j]

    lat = jnp.concatenate([(tok[r].astype(F32) + tokh[r].astype(F32)).astype(BF16) for r in range(n_seq)], axis=0)
    split = dot(lat, spread[...], 1, 0)
    stack = jnp.concatenate(
        [
            jnp.concatenate([split[r * cl : (r + 1) * cl, q * n : (q + 1) * n] for r in range(n_seq)], axis=1)
            for q in range(PATCH)
        ],
        axis=0,
    )
    tg_t = dot(order, stack.astype(BF16), 1, 0)
    facc[...] = dot(tg_t.astype(BF16), nb[...], 1, 0)
    column = jnp.sum(tg_t, axis=1, keepdims=True)
    tgs[...] = tg_t.T.astype(BF16)

    fw = fw_ref[...].astype(F32)
    macc[0:1] = jnp.sum(fw * column, axis=0, keepdims=True)
    macc[1:2] = jnp.sum(fw * facc[...], axis=0, keepdims=True)
    facc[...] = facc[...] * scale + column * shift

    pieces = d_model // chans
    small = jnp.concatenate(
        [misc[0 : TAPS * cl + 1, :]]
        + [macc[b : b + 1, p * chans : (p + 1) * chans] for b in range(2) for p in range(pieces)]
        + [jnp.zeros((e - TAPS * cl - 1 - 2 * pieces, chans), F32)],
        axis=0,
    )
    nc, er, cwc = f4.shape[0], f4.shape[3], f4.shape[4]
    for a, c, k, lo, mid, end in places(n_tm, e // er, nc, cwc, d_model, chans):
        at = slice(k * er, (k + 1) * er)
        to = f4.at[c, a % CORES, a // CORES]
        if mid > lo:
            to[:, : mid - lo] = facc[at, lo:mid].astype(BF16)
        if end > mid:
            to[:, mid - lo : end - lo] = small[at, mid - d_model : end - d_model].astype(BF16)
        if lo + cwc > end:
            to[:, end - lo :] = jnp.zeros((er, lo + cwc - end), BF16)
    chunks = range(nc)
    f_core = [copy(f4.at[c, other], fcore.at[c], s_fc.at[c], r_fc.at[c], sibling) for c in chunks]
    for c in chunks:
        f_core[c].start()

    half = hid.shape[0] // 2

    def input_gradient(k):
        at = slice(k * half, (k + 1) * half)
        normed = nb[at, :].astype(F32)
        ng = dot(tgs[at, :], fw_ref[...], 1, 0) * scale
        m1 = jnp.mean(ng, axis=1, keepdims=True)
        m2 = jnp.mean(ng * normed, axis=1, keepdims=True)
        dx_ref[at, :] = (inv[at, 0:1] * (ng - m1 - normed * m2)).astype(BF16)

    f_xy = [
        [
            copy(fhalf.at[c, p], frecv.at[c, d - 1], s_f.at[c, d - 1], r_f.at[c, d - 1], (p * CORES + core, j))
            for d, p in tms
        ]
        for c in chunks
    ]
    f_z = [
        [copy(fall.at[c, j], fall.at[c, j], s_f2.at[c, d - 1], r_f2.at[c, d - 1], (i, p)) for d, p in seqs]
        for c in chunks
    ]
    g_xy = [
        [
            copy(
                gath.at[c, core, chip], gath.at[c, core, chip], s_g.at[c, d - 1], r_g.at[c, d - 1],
                (p * CORES + core, j),
            )
            for d, p in tms
        ]
        for c in chunks
    ]
    g_core = [copy(gath.at[c, core], gath.at[c, core], s_gc.at[c], r_gc.at[c], sibling) for c in chunks]

    def start(copies):
        for c in copies:
            c.start()

    def wait(copies):
        for c in copies:
            c.wait()

    def final_xy(c):
        f_core[c].wait()
        for q in range(chips):
            fhalf[c, q] = (f4[c, core, q].astype(F32) + fcore[c, q].astype(F32)).astype(BF16)
        start(f_xy[c])

    def final_z(c):
        wait(f_xy[c])
        total = fhalf[c, chip].astype(F32)
        for k in range(chips - 1):
            total = total + frecv[c, k].astype(F32)
        fall[c, j] = total.astype(BF16)
        start(f_z[c])

    def gather_xy(c):
        wait(f_z[c])
        total = fall[c, 0].astype(F32)
        for k in range(1, n_seq):
            total = total + fall[c, k].astype(F32)
        gath[c, core, chip] = total.astype(BF16)
        start(g_xy[c])

    def gather_core(c):
        wait(g_xy[c])
        g_core[c].start()

    weight(2)
    w_core[2].start()
    for c in chunks:
        final_xy(c)
    weight_z(0)
    input_gradient(0)
    input_gradient(1)
    for c in chunks:
        final_z(c)
    weight_xy(2)
    for c in chunks:
        gather_xy(c)
    weight_end(0)
    weight_z(1)
    weight_z(2)
    for c in chunks:
        gather_core(c)
    weight_end(1)
    weight_end(2)
    wait(g_core)


def unpack_kernel(gath, wg_ref, dx_in, fin_ref, mod_ref, in_ref, bias_ref, wg_out, dx_hbm, small, sem):
    part = dx_in.shape[0] // sem.shape[0]
    dx_copies = [
        pltpu.make_async_copy(dx_in.at[pl.ds(k * part, part)], dx_hbm.at[pl.ds(k * part, part)], sem.at[k])
        for k in range(sem.shape[0])
    ]
    for c in dx_copies:
        c.start()
    nc, cores, chips, er, cwc = gath.shape
    n_tm = cores * chips
    d_model = fin_ref.shape[1]
    taps_cl, chans = in_ref.shape
    pieces = d_model // chans
    for a, c, k, lo, mid, end in places(n_tm, fin_ref.shape[0] // er, nc, cwc, d_model, chans):
        at = slice(k * er, (k + 1) * er)
        part = gath.at[c, a % cores, a // cores]
        if mid > lo:
            fin_ref[at, lo:mid] = part[:, : mid - lo].astype(F32)
        if end > mid:
            small[at, mid - d_model : end - d_model] = part[:, mid - lo : end - lo].astype(F32)
    in_ref[...] = small[:taps_cl, :]
    bias_ref[...] = small[taps_cl : taps_cl + 1, :]
    for b in range(2):
        for p in range(pieces):
            at = taps_cl + 1 + b * pieces + p
            mod_ref[b : b + 1, p * chans : (p + 1) * chans] = small[at : at + 1, :]
    wg_out[...] = wg_ref[...]
    for c in dx_copies:
        c.wait()


def local(n_tm, n_seq, latents, hidden, grad_out, conv_in_w, conv_in_b, conv_w, final_w, modulation, clip_start):
    slab, cl, width = latents.shape
    taps, chans = conv_w.shape[:2]
    tokens, d_model = hidden.shape
    rows = chans // (n_tm * n_seq)
    block = n_seq * rows
    chips = n_tm // CORES
    w_in = conv_in_w.transpose(0, 2, 1).reshape(taps * cl, chans)
    bias = conv_in_b.reshape(1, chans)
    e = cl * PATCH
    er = 16
    parts = n_tm // (e // er)
    lanes = -(-(d_model + chans) // (parts * 128))
    nc = max(c for c in range(1, CHUNKS + 1) if lanes % c == 0)
    cw = lanes // nc * 128
    vmem = pl.BlockSpec(memory_space=pltpu.VMEM)
    hbm = pl.BlockSpec(memory_space=pltpu.HBM)
    smem = pl.BlockSpec(memory_space=pltpu.SMEM)
    dma = pltpu.SemaphoreType.DMA
    nt, ns = chips - 1, n_seq - 1

    def b16(*shape):
        return pltpu.VMEM(shape, BF16)

    def f32(*shape):
        return pltpu.VMEM(shape, F32)

    def in_hbm(x):
        return pltpu.with_memory_space_constraint(x, pltpu.HBM)

    dx, wg, gath = pl.pallas_call(
        functools.partial(main_kernel, n_tm, n_seq),
        out_shape=(
            b16(tokens, d_model),
            f32(taps, rows, chans),
            b16(nc, CORES, chips, er, cw),
        ),
        in_specs=[hbm] * 9,
        out_specs=(vmem, vmem, vmem),
        scratch_shapes=[
            pltpu.SMEM(clip_start.shape, jnp.int32),
            b16(taps * cl, chans),
            f32(1, chans),
            b16(e, d_model),
            f32(2, d_model),
            b16(slab + HALO, cl, width),
            b16(slab, cl, width),
            f32(slab + 2 - HALO, chans, width),
            b16(slab, chans, width),
            b16(tokens, d_model),
            b16(tokens, d_model),
            f32(tokens, 128),
            b16(chans, 4 * cl),
            b16(slab + 2, 4 * cl, width),
            b16(taps + 3, chans, chans),
            b16(slab + 2, chans, width),
            f32(slab + 2, chans, width),
            b16(slab + 2, chans, width),
            f32(slab + 2, taps * cl, width),
            f32(4 * cl, chans),
            f32(slab + HALO, cl, width),
            b16(HALO, cl, width),
            b16(slab, cl, width),
            b16(n_seq, cl, width),
            b16(n_seq, cl, width),
            b16(taps, CORES, chips, block, chans),
            b16(taps, chips, block, chans),
            b16(taps, chips, block, chans),
            b16(taps, nt, block, chans),
            b16(taps, n_seq, rows, chans),
            b16(taps, ns, rows, chans),
            b16(width, width),
            b16(tokens, e),
            f32(e, d_model),
            f32(8, d_model),
            b16(nc, CORES, chips, er, cw),
            b16(nc, chips, er, cw),
            b16(nc, chips, er, cw),
            b16(nc, nt, er, cw),
            b16(nc, n_seq, er, cw),
            dma((9,)), dma((slab,)), dma(()), dma(()), dma((n_seq,)), dma((n_seq,)), dma((ns,)), dma((ns,)),
            dma((taps,)), dma((taps,)), dma((taps, nt)), dma((taps, nt)), dma((taps, ns)), dma((taps, ns)),
            dma((nc,)), dma((nc,)), dma((nc, nt)), dma((nc, nt)), dma((nc, ns)), dma((nc, ns)),
            dma((nc, nt)), dma((nc, nt)), dma((nc,)), dma((nc,)),
        ],
        compiler_params=pltpu.CompilerParams(
            vmem_limit_bytes=MAIN_VMEM, collective_id=0, has_side_effects=True
        ),
        name="main",
    )(*[in_hbm(x) for x in (clip_start, latents, hidden, grad_out, w_in, bias, conv_w, final_w.T, modulation)])
    fin, mod, w_in_grad, bias_grad, wg, dx = pl.pallas_call(
        unpack_kernel,
        out_shape=(
            jax.ShapeDtypeStruct((e, d_model), F32),
            jax.ShapeDtypeStruct((2, d_model), F32),
            jax.ShapeDtypeStruct((taps * cl, chans), F32),
            jax.ShapeDtypeStruct((1, chans), F32),
            jax.ShapeDtypeStruct((taps, rows, chans), F32),
            jax.ShapeDtypeStruct((tokens, d_model), BF16),
        ),
        in_specs=[vmem, vmem, vmem],
        out_specs=(vmem,) * 5 + (hbm,),
        scratch_shapes=[f32(e, chans), dma((4,))],
        compiler_params=pltpu.CompilerParams(vmem_limit_bytes=SMALL_VMEM),
        name="unpack",
    )(gath, wg, dx)
    return (
        dx,
        wg.transpose(1, 0, 2),
        w_in_grad.reshape(taps, cl, chans).transpose(0, 2, 1),
        bias_grad.reshape(chans),
        fin.T,
        mod,
    )


def solution(mesh):
    return jax.shard_map(
        functools.partial(local, mesh.shape["tm"], mesh.shape["seq"]),
        mesh=mesh,
        in_specs=(
            P("tm", None, "seq"),
            P(("tm", "seq"), None),
            P("tm", None, "seq"),
            P(),
            P(),
            P(),
            P(),
            P(),
            P(),
        ),
        out_specs=(P(("tm", "seq"), None), P(("tm", "seq"), None, None), P(), P(), P(), P()),
        check_vma=False,
    )
```
